32 devices in a mesh: dp: 4 (over y, x), hidden: 8 (over z, core).
Axes of the slice: x: 2, y: 2, z: 4, core: 2. Of those that a mesh axis runs over, the one named last changes fastest.
Arguments:
- tokens: bfloat16 [2048, 6144], P('dp', 'hidden'), as said below
- cotangent: bfloat16 [2048, 6144], P('dp', 'hidden'), may hold values from -6 to 6
- weight_in: bfloat16 [6144, 3072], P('hidden'), may hold values from -0.21875 to 0.21875
- level_weights: bfloat16 [3, 192, 2, 128, 128], P(None, 'hidden'), may hold values from -0.375 to 0.375
- weight_out: bfloat16 [24576, 768], P('hidden'), may hold values from -0.109375 to 0.109375
- block_order: int32 [3, 24], replicated, may hold values from 0 to 23, each once within a row
Outputs:
- branch_output: bfloat16 [2048, 6144], P('dp', 'hidden')
- token_grad: bfloat16 [2048, 6144], P('dp', 'hidden')
- level_grad: float32 [3, 192, 2, 128, 128], P(None, 'hidden', None, 'dp')
- input_grad: float32 [6144, 3072], P(('hidden', 'dp'))
- output_grad: float32 [24576, 768], P(('hidden', 'dp'))
The draws below stay inside these ranges and needn't reach their ends.
Inputs may be any that keep to these rules, and one draw needn't show every extreme that they name: Each row of block_order lists every number from 0 to 23 once. `tokens`: entries are finite.
All inputs are finite; a program needn't handle non-finite values.
Results may differ from the reference program's by a relative error of at most 0.017.
Values may be sent and summed in bfloat16 or wider, within the bound.
A program may use at most 192 MiB of HBM per device.

```python
import math
import jax
import jax.numpy as jnp
from jax import lax

D = 6144
FF = 24576
BLK = 128
TOK_DEV = 512
LEVELS = 3
BF = 24
NBF = 192
TOKENS = 2048
N_DP = 4
N_HIDDEN = 8


def draw_tokens(key, part):
    first, second, third = jax.random.split(key, 3)
    column = jnp.arange(D, dtype=jnp.float32) / D
    base = jax.random.normal(first, (TOKENS, D), jnp.float32)
    rising = jnp.exp(column * math.log(3.0))
    column_scale = rising * jnp.exp(jax.random.uniform(second, (D,), jnp.float32, 0.0, math.log(4.0)))
    row_scale = jnp.exp(jax.random.uniform(third, (TOKENS, 1), jnp.float32, 0.0, math.log(10.0)))
    return (base * column_scale * row_scale).astype(jnp.bfloat16)


def block_levels(rng, shape, cuts, smallest, high):
    def one(axis_at, parts):
        heights = jax.random.uniform(jax.random.fold_in(jax.random.fold_in(rng, 6), axis_at), (parts,), jnp.float32, smallest / len(cuts), high / len(cuts))
        return jnp.repeat(jnp.exp(heights), shape[axis_at] // parts).reshape((-1,) + (1,) * (len(shape) - axis_at - 1))

    gain = one(*cuts[0])
    for cut in cuts[1:]:
        gain = gain * one(*cut)
    return gain


def normal_values(stream_key, shape, spread, most, shards=(), kind=jnp.bfloat16):
    result = spread * jax.random.normal(stream_key, shape, jnp.float32)
    if shards:
        result = result * block_levels(stream_key, shape, shards, -0.22, 0.18)
    return jnp.clip(result, -most, most).astype(kind)


def setup_inputs(seed: int = 0) -> dict:
    seeds = jax.random.split(jax.random.key(seed), 7)
    return {
        "tokens": draw_tokens(jax.random.fold_in(seeds[6], 71), 0),
        "cotangent": normal_values(seeds[1], (TOKENS, D), 1.0, 6.0, ((0, 4), (1, 8))),
        "weight_in": normal_values(seeds[2], (D, FF // N_HIDDEN), (D // N_HIDDEN) ** -0.5, 0.21875, ((0, 8),)),
        "level_weights": normal_values(seeds[3], (LEVELS, NBF, 2, BLK, BLK), (2 * BLK) ** -0.5, 0.375, ((1, 8),)),
        "weight_out": normal_values(seeds[4], (FF, D // N_HIDDEN), (FF // N_HIDDEN) ** -0.5, 0.109375, ((0, 8),)),
        "block_order": jax.vmap(lambda own: jax.random.permutation(own, BF))(jax.random.split(seeds[5], LEVELS)).reshape((LEVELS, BF)).astype(jnp.int32),
    }


def flip_pairs(values, level_index):
    shape = values.shape
    split = values.reshape(shape[0], shape[1] >> level_index + 1, 2, 1 << level_index, shape[2], shape[3])
    return split[:, :, ::-1].reshape(shape)

def reference(tokens, cotangent, weight_in, level_weights, weight_out, block_order):
    wide = jnp.float32
    groups = N_HIDDEN
    width_local = D // N_HIDDEN
    units_local = FF // N_HIDDEN
    weights_first = weight_in.astype(wide).reshape(groups, width_local, units_local)
    weights_last = weight_out.astype(wide).reshape(groups, units_local, width_local)
    butterfly = level_weights.astype(wide).reshape(LEVELS, groups, BF, 2, BLK, BLK)
    positions = jnp.broadcast_to(jnp.arange(BF, dtype=jnp.int32), (LEVELS, BF))
    inverse = jnp.zeros_like(block_order).at[jnp.arange(LEVELS)[:, None], block_order].set(positions)
    grad_scale = 1.0 / math.sqrt(TOKENS)

    def one_block(carry, pieces):
        level_acc, first_acc, last_acc = carry
        tok_block, cot_block = pieces
        row_count = tok_block.shape[0]
        tokens_wide = tok_block.astype(wide)
        recip_rms = lax.rsqrt(lax.optimization_barrier(jnp.mean(tokens_wide * tokens_wide, axis=1, keepdims=True)) + 1e-06)
        normed = (tokens_wide * recip_rms).astype(jnp.bfloat16)
        normed_groups = normed.astype(wide).reshape(row_count, groups, width_local)
        current = jnp.einsum('rpc,pcf->rpf', normed_groups, weights_first).astype(jnp.bfloat16)
        current = current.reshape(row_count, groups, BF, BLK)
        inputs_kept = []
        partner_kept = []
        for level_index in range(LEVELS):
            shifted = flip_pairs(current, level_index)[:, :, block_order[level_index]]
            mixed_out = jnp.einsum('rpjc,pjcd->rpjd', current.astype(wide), butterfly[level_index, :, :, 0])
            mixed_out = mixed_out + jnp.einsum('rpjc,pjcd->rpjd', shifted.astype(wide), butterfly[level_index, :, :, 1])
            inputs_kept.append(current)
            partner_kept.append(shifted)
            current = mixed_out.astype(jnp.bfloat16)
        top_layer = current.astype(wide).reshape(row_count, groups, units_local)
        activated = jax.nn.gelu(top_layer).astype(jnp.bfloat16).astype(wide)
        result_out = jnp.einsum('rpf,pfd->rpd', activated, weights_last).astype(jnp.bfloat16)
        cot_groups = cot_block.astype(wide).reshape(row_count, groups, width_local)
        last_grad = jnp.einsum('rpf,rpd->pfd', activated, cot_groups) * grad_scale
        d_hidden = jnp.einsum('rpd,pfd->rpf', cot_groups, weights_last)
        _, pullback = jax.vjp(jax.nn.gelu, top_layer)
        upstream = pullback(d_hidden)[0].astype(jnp.bfloat16).reshape(row_count, groups, BF, BLK)
        level_list = [None] * LEVELS
        for level_index in reversed(range(LEVELS)):
            upstream_wide = upstream.astype(wide)
            grad_own = jnp.einsum('rpjc,rpjd->pjcd', inputs_kept[level_index].astype(wide), upstream_wide)
            grad_partner = jnp.einsum('rpjc,rpjd->pjcd', partner_kept[level_index].astype(wide), upstream_wide)
            level_list[level_index] = jnp.stack([grad_own, grad_partner], axis=2) * grad_scale
            own_term = jnp.einsum('rpjd,pjcd->rpjc', upstream_wide, butterfly[level_index, :, :, 0])
            sent_term = jnp.einsum('rpjd,pjcd->rpjc', upstream_wide, butterfly[level_index, :, :, 1]).astype(jnp.bfloat16)
            placed = flip_pairs(sent_term, level_index)[:, :, inverse[level_index]]
            upstream = (own_term + placed.astype(wide)).astype(jnp.bfloat16)
        flat_grad = upstream.astype(wide).reshape(row_count, groups, units_local)
        first_grad = jnp.einsum('rpc,rpf->pcf', normed_groups, flat_grad) * grad_scale
        d_normed = jnp.einsum('rpf,pcf->rpc', flat_grad, weights_first).reshape(row_count, D)
        inner_mean = lax.optimization_barrier(jnp.mean(d_normed * tokens_wide, axis=1, keepdims=True))
        token_out = (recip_rms * d_normed - tokens_wide * recip_rms * recip_rms * recip_rms * inner_mean).astype(jnp.bfloat16)
        new_carry = (level_acc + jnp.stack(level_list), first_acc + first_grad, last_acc + last_grad)
        return (new_carry, (result_out.reshape(row_count, D), token_out))
    start = (jnp.zeros((LEVELS, groups, BF, 2, BLK, BLK), wide), jnp.zeros((groups, width_local, units_local), wide), jnp.zeros((groups, units_local, width_local), wide))
    pieces = (tokens.reshape(N_DP, TOK_DEV, D), cotangent.reshape(N_DP, TOK_DEV, D))
    totals, outputs = lax.scan(one_block, start, pieces)
    branch_output = outputs[0].reshape(TOKENS, D)
    token_grad = outputs[1].reshape(TOKENS, D)
    level_grad = totals[0].reshape(LEVELS, NBF, 2, BLK, BLK)
    input_grad = totals[1].reshape(D, units_local)
    output_grad = totals[2].reshape(FF, width_local)
    return (branch_output, token_grad, level_grad, input_grad, output_grad)
```

```python
import functools
import math

import jax
import jax.numpy as jnp
from jax import lax
from jax.experimental import pallas as pl
from jax.experimental.pallas import tpu as pltpu
from jax.sharding import PartitionSpec as P

WIDE = jnp.float32
NARROW = jnp.bfloat16
MESH = pl.DeviceIdType.MESH
ROWS = 128
SUB = 8


def dot(a, b, dims):
    return lax.dot_general(a, b, (dims, ((), ())), preferred_element_type=WIDE)


def nn(a, b):
    return dot(a, b, ((1,), (0,)))


def nt(a, b):
    return dot(a, b, ((1,), (1,)))


def tn(a, b):
    return dot(a, b, ((0,), (0,)))


def gelu_pair(v):
    c = math.sqrt(2.0 / math.pi)
    square = v * v
    t = jnp.tanh(c * v * (1.0 + 0.044715 * square))
    half = 0.5 * (1.0 + t)
    slope = half + 0.5 * v * (1.0 - t * t) * c * (1.0 + 3.0 * 0.044715 * square)
    return v * half, slope


def schedule(levels, chunks):
    steps = {}

    def add(step, wish, *needs):
        steps[step] = (wish, needs)

    for c in range(chunks):
        add(("start", 0, c), c)
        for k in range(levels):
            before = ("start", 0, c) if k == 0 else ("forward", k - 1, c)
            wish = c + 1.5 if k == 0 else 10 + 2 * c + 3 * (k - 1) + (0 if k < levels - 1 else 2 * c)
            add(("forward", k, c), wish, before)
        add(("output", 0, c), 10 + 4 * c + 3 * levels, ("forward", levels - 1, c))
    top = 100
    done = [("forward", levels - 1, c) for c in range(chunks)]
    add(("output_grad", 0, 0), top, *done, *[("output", 0, c) for c in range(chunks)])
    for k in reversed(range(levels)):
        made = [("forward", levels - 1, c) if k == levels - 1 else ("backward", k + 1, c) for c in range(chunks)]
        deep = levels - 1 - k
        add(("level_grad", k, 0), top + 2 * deep + 2 * chunks - 1.5 if deep else top + 0.5, *made)
        for c in range(chunks):
            needs = [made[c], ("output_grad", 0, 0)]
            if k + 2 <= levels:
                needs.append(("level_grad", k + 1, 0))
            add(("backward", k, c), top + 1 + 2 * c + 2.5 * deep, *needs)
    order = []
    left = dict(steps)
    while left:
        ready = [s for s, (_, needs) in left.items() if not any(n in left for n in needs)]
        pick = min(ready, key=lambda s: left[s][0])
        order.append(pick)
        del left[pick]
    return order


def layer(
    plan,
    order,
    inverse,
    tokens,
    cotangent,
    weight_in,
    level_weights,
    weight_out,
    out_hbm,
    token_grad_hbm,
    level_parts,
    in_parts,
    out_parts,
    *scratch,
):
    L, N, C, T, Dl, NB, total_features = plan
    scratch = list(scratch)

    def take(count):
        taken = scratch[:count]
        del scratch[:count]
        return taken

    U = take(L)
    R = [take(C) for _ in range(L)]
    S = take(2)
    Tt = [take(C) for _ in range(2)]
    G = take(2)
    tok, cot, w_in, lw, w_out = take(5)
    recip, norm_t, xs, dn, acc, ost, lg = take(7)
    squares, squares_in, inner, inner_in = take(4)
    load_sem, fs, fr, bs, br, ps, pr, rs, rr, own_sem, credit, store_sem = take(12)
    act = S[1]

    hidden = lax.axis_index("hidden")
    dp = lax.axis_index("dp")
    partner = []
    for k in range(L):
        mask = 2**k
        bit = lax.rem(hidden // mask, 2)
        partner.append(hidden + mask - 2 * mask * bit)
    peers = [lax.rem(dp + off, N) for off in range(1, N)]

    barrier = pltpu.get_barrier_semaphore()
    for p in partner:
        pl.semaphore_signal(barrier, inc=1, device_id={"hidden": p}, device_id_type=MESH)
    for p in peers:
        pl.semaphore_signal(barrier, inc=1, device_id={"dp": p}, device_id_type=MESH)

    loads = [
        pltpu.make_async_copy(src, dst, load_sem.at[i])
        for i, (src, dst) in enumerate(
            ((tokens, tok), (weight_in, w_in), (level_weights, lw), (cotangent, cot), (weight_out, w_out))
        )
    ]
    for load in loads:
        load.start()
    loaded = set()

    def need(*which):
        for i in which:
            if i not in loaded:
                loaded.add(i)
                loads[i].wait()

    def to_hidden(src, dst, send, recv, k):
        return pltpu.make_async_remote_copy(
            src_ref=src,
            dst_ref=dst,
            send_sem=send,
            recv_sem=recv,
            device_id={"hidden": partner[k]},
            device_id_type=MESH,
        )

    def forward_copy(k, c):
        return to_hidden(U[k].at[c], R[k][c], fs.at[k, c], fr.at[k, c], k)

    def backward_copy(k, c):
        way = (L - 1 - k) % 2
        return to_hidden(S[way].at[c], Tt[way][c], bs.at[k, c], br.at[k, c], k)

    def sum_copy(i, k, mine, inbox):
        return to_hidden(mine.at[k], inbox.at[k], ps.at[i, k], pr.at[i, k], k)

    def to_dp(i, off, src, dst):
        return pltpu.make_async_remote_copy(
            src_ref=src,
            dst_ref=dst,
            send_sem=rs.at[i, off - 1],
            recv_sem=rr.at[i, off - 1],
            device_id={"dp": peers[off - 1]},
            device_id_type=MESH,
        )

    out_share, in_share = out_parts.shape[1], in_parts.shape[1]

    def level_copy(k, off):
        return to_dp(k, off, lg.at[k, peers[off - 1]], level_parts.at[k, off])

    def in_rows(at):
        return pl.ds(pl.multiple_of(at * in_share, 16), in_share)

    def out_rows(at):
        return pl.ds(pl.multiple_of(at * out_share, 16), out_share)

    def in_copy(off):
        return to_dp(L, off, w_in.at[in_rows(peers[off - 1])], in_parts.at[off])

    def out_copy(off):
        return to_dp(L + 1, off, w_out.at[out_rows(peers[off - 1])], out_parts.at[off])

    own_copies = [pltpu.make_async_copy(lg.at[k, dp], level_parts.at[k, 0], own_sem.at[k]) for k in range(L)]
    own_copies.append(pltpu.make_async_copy(w_in.at[in_rows(dp)], in_parts.at[0], own_sem.at[L]))
    own_copies.append(pltpu.make_async_copy(w_out.at[out_rows(dp)], out_parts.at[0], own_sem.at[L + 1]))

    def rows(c):
        return pl.ds(c * ROWS, ROWS)

    def as_row(column):
        return jnp.broadcast_to(column, (ROWS, ROWS)).T[:SUB]

    def as_column(row):
        return jnp.broadcast_to(row[:1], (ROWS, ROWS)).T

    def pairs(body):
        def step(i, carry):
            body(i)
            return carry

        lax.fori_loop(0, NB // 2, step, 0)

    def wide_columns(i, width):
        return pl.ds(pl.multiple_of(i * width, width), width)

    need(0)
    for c in range(C):
        x = tok[rows(c), :].astype(WIDE)
        squares[0, :, rows(c)] = as_row(jnp.sum(x * x, axis=1, keepdims=True))
    pl.semaphore_wait(barrier, L + N - 1)
    for k in range(L):
        copy = sum_copy(0, k, squares, squares_in)
        copy.start()
        copy.wait()
        squares[k + 1] = squares[k] + squares_in[k]
    for c in range(C):
        mean = squares[L, :, rows(c)] / total_features
        recip[rows(c), :] = as_column(lax.rsqrt(mean + 1e-06))

    def start(_, c):
        need(1)
        x = (tok[rows(c), :].astype(WIDE) * recip[rows(c), :1]).astype(NARROW)
        xs[...] = x
        norm_t[:, rows(c)] = x.astype(WIDE).T.astype(NARROW)

        def body(i):
            wide = nn(xs[...], w_in[:, wide_columns(i, 256)]).astype(NARROW)
            U[0][c, 2 * i] = wide[:, :128]
            U[0][c, 2 * i + 1] = wide[:, 128:]

        pairs(body)
        forward_copy(0, c).start()

    def mixed(k, c, j):
        both = jnp.concatenate([U[k][c, j], R[k][c][order[k, j]]], axis=1)
        return nn(both, lw[k, j].reshape(256, 128)).astype(NARROW)

    def forward(k, c):
        need(2)
        forward_copy(k, c).wait_recv()
        if k < L - 1:

            def body(i):
                for j in (2 * i, 2 * i + 1):
                    U[k + 1][c, j] = mixed(k, c, j)

            pairs(body)
            forward_copy(k + 1, c).start()
            return
        need(3, 4)

        def body(i):
            d_act = nt(cot[rows(c), :], w_out[wide_columns(i, 256), :])
            for b in range(2):
                j = 2 * i + b
                value, slope = gelu_pair(mixed(k, c, j).astype(WIDE))
                act[c, j] = value.astype(NARROW)
                g = (d_act[:, b * 128 : (b + 1) * 128] * slope).astype(NARROW)
                G[0][c, j] = g
                S[0][c, j] = nt(g, lw[k, j, 1]).astype(NARROW)

        pairs(body)
        backward_copy(k, c).start()

    def output(_, c):
        acc[...] = jnp.zeros_like(acc)

        def step(q, carry):
            wide = jnp.concatenate([act[c, 4 * q + b] for b in range(4)], axis=1)
            acc[...] += nn(wide, w_out[wide_columns(q, 512), :])
            return carry

        lax.fori_loop(0, NB // 4, step, 0)
        ost[rows(c), :] = acc[...].astype(NARROW)

    def all_rows(ref, j):
        return jnp.concatenate([ref[c, j] for c in range(C)], axis=0)

    def all_pair(ref, i):
        return jnp.concatenate([all_rows(ref, 2 * i), all_rows(ref, 2 * i + 1)], axis=1)

    out_store = pltpu.make_async_copy(ost, out_hbm, store_sem.at[0])
    token_store = pltpu.make_async_copy(tok, token_grad_hbm, store_sem.at[1])

    def output_grad(_, __):
        out_store.start()

        def body(i):
            w_out[wide_columns(i, 256), :] = tn(all_pair(act, i), cot[...]).astype(NARROW)

        pairs(body)
        for off in range(1, N):
            out_copy(off).start()
        own_copies[L + 1].start()

    def level_grad(k, _):
        share = 128 // N

        def step(j, carry):
            theirs = jnp.concatenate([R[k][c][order[k, j]] for c in range(C)], axis=0)
            both = jnp.concatenate([all_rows(U[k], j), theirs], axis=1)
            value = tn(both, all_rows(G[(L - 1 - k) % 2], j)).astype(NARROW)
            for r in range(N):
                for b in range(2):
                    lg[k, r, j, b] = value[b * 128 + r * share : b * 128 + (r + 1) * share]
            return carry

        lax.fori_loop(0, NB, step, 0)
        for off in range(1, N):
            level_copy(k, off).start()
        own_copies[k].start()

    def backward(k, c):
        backward_copy(k, c).wait_recv()
        if 0 < k < L - 1:
            backward_copy(k + 1, c).wait_send()
        upper, lower = G[(L - 1 - k) % 2], G[(L - k) % 2]
        came = Tt[(L - 1 - k) % 2][c]
        send = S[(L - k) % 2]

        def body(i):
            for j in (2 * i, 2 * i + 1):
                g = (nt(upper[c, j], lw[k, j, 0]) + came[inverse[k, j]].astype(WIDE)).astype(NARROW)
                lower[c, j] = g
                if k > 0:
                    send[c, j] = nt(g, lw[k - 1, j, 1]).astype(NARROW)

        pairs(body)
        if k >= 2:
            pl.semaphore_signal(
                credit.at[k - 2, c], inc=1, device_id={"hidden": partner[k - 2]}, device_id_type=MESH
            )
        if k > 0:
            if k - 1 <= L - 3:
                pl.semaphore_wait(credit.at[k - 1, c], 1)
            backward_copy(k - 1, c).start()
            return
        dn[rows(c), :] = jnp.zeros((ROWS, Dl), WIDE)

        def step(q, carry):
            wide = jnp.concatenate([lower[c, 4 * q + b] for b in range(4)], axis=1)
            dn[rows(c), :] += nt(wide, w_in[:, wide_columns(q, 512)])
            return carry

        lax.fori_loop(0, NB // 4, step, 0)
        dot_rows = jnp.sum(dn[rows(c), :] * tok[rows(c), :].astype(WIDE), axis=1, keepdims=True)
        inner[0, :, rows(c)] = as_row(dot_rows)

    doing = dict(
        start=start,
        forward=forward,
        output=output,
        output_grad=output_grad,
        level_grad=level_grad,
        backward=backward,
    )
    for name, k, c in schedule(L, C):
        doing[name](k, c)

    first = G[L % 2]

    def in_grad(at):
        def body(i):
            w_in[in_rows(at), wide_columns(i, 256)] = nn(norm_t[in_rows(at), :], all_pair(first, i)).astype(NARROW)

        pairs(body)

    sum_copy(1, 0, inner, inner_in).start()
    for off in range(1, max(N, L) + 1):
        if off <= N:
            in_grad(peers[off - 1] if off < N else dp)
            (in_copy(off) if off < N else own_copies[L]).start()
        hop = off - 1
        if hop < L:
            sum_copy(1, hop, inner, inner_in).wait()
            inner[hop + 1] = inner[hop] + inner_in[hop]
            if hop + 1 < L:
                sum_copy(1, hop + 1, inner, inner_in).start()
    for c in range(C):
        mean = as_column(inner[L, :, rows(c)] / total_features)[:, :1]
        scale = recip[rows(c), :1]
        cube = scale * scale * scale
        wide = tok[rows(c), :].astype(WIDE)
        tok[rows(c), :] = (scale * dn[rows(c), :] - wide * (cube * mean)).astype(NARROW)
    token_store.start()

    for k in range(L):
        for c in range(C):
            forward_copy(k, c).wait_send()
            if k < 2:
                backward_copy(k, c).wait_send()
    for off in range(1, N):
        for k in range(L):
            level_copy(k, off).wait()
        out_copy(off).wait()
        in_copy(off).wait()
    for copy in own_copies:
        copy.wait()
    out_store.wait()
    token_store.wait()


def local(sizes, tokens, cotangent, weight_in, level_weights, weight_out, block_order):
    N, H = sizes
    T, Dl = tokens.shape
    L, NB = block_order.shape
    F = weight_in.shape[1]
    BLK = level_weights.shape[-1]
    C = T // ROWS
    grad_scale = 1.0 / math.sqrt(T * N)
    seats = jnp.arange(NB, dtype=jnp.int32)
    inverse = jnp.sum(
        jnp.where(block_order[:, :, None] == seats[None, None, :], seats[None, :, None], 0), axis=1, dtype=jnp.int32
    )
    slab = pltpu.VMEM((C, NB, ROWS, BLK), NARROW)
    piece = pltpu.VMEM((NB, ROWS, BLK), NARROW)
    scratch = [slab] * L + [piece] * (L * C) + [slab] * 2 + [piece] * (2 * C) + [slab] * 2
    scratch += [
        pltpu.VMEM(a.shape, a.dtype) for a in (tokens, cotangent, weight_in, level_weights, weight_out)
    ]
    scratch += [
        pltpu.VMEM((T, ROWS), WIDE),
        pltpu.VMEM((Dl, T), NARROW),
        pltpu.VMEM((ROWS, Dl), NARROW),
        pltpu.VMEM((T, Dl), WIDE),
        pltpu.VMEM((ROWS, Dl), WIDE),
        pltpu.VMEM((T, Dl), NARROW),
        pltpu.VMEM((L, N, NB, 2, BLK // N, BLK), NARROW),
    ]
    scratch += [pltpu.VMEM((count, SUB, T), WIDE) for count in (L + 1, L, L + 1, L)]
    dma = pltpu.SemaphoreType.DMA
    scratch += [dma((5,))] + [dma((L, C))] * 4 + [dma((2, L))] * 2 + [dma((L + 2, N - 1))] * 2 + [dma((L + 2,))]
    scratch += [pltpu.SemaphoreType.REGULAR((max(L - 2, 1), C)), dma((2,))]
    outs = (
        jax.ShapeDtypeStruct((T, Dl), NARROW),
        jax.ShapeDtypeStruct((T, Dl), NARROW),
        jax.ShapeDtypeStruct((L, N, NB, 2, BLK // N, BLK), NARROW),
        jax.ShapeDtypeStruct((N, Dl // N, F), NARROW),
        jax.ShapeDtypeStruct((N, F // N, Dl), NARROW),
    )
    plan = (L, N, C, T, Dl, NB, Dl * H)
    result, token_grad, level_parts, in_parts, out_parts = pl.pallas_call(
        functools.partial(layer, plan),
        out_shape=outs,
        in_specs=[pl.BlockSpec(memory_space=pltpu.SMEM)] * 2 + [pl.BlockSpec(memory_space=pl.ANY)] * 5,
        out_specs=[pl.BlockSpec(memory_space=pl.ANY)] * 5,
        scratch_shapes=scratch,
        compiler_params=pltpu.CompilerParams(
            collective_id=0, has_side_effects=True, vmem_limit_bytes=63 * 2**20
        ),
        cost_estimate=pl.CostEstimate(flops=18 * T * Dl * F, bytes_accessed=30 * 2**20, transcendentals=T * F),
    )(block_order, inverse, tokens, cotangent, weight_in, level_weights, weight_out)

    def total(parts, axis):
        return jnp.sum(parts.astype(WIDE), axis=axis) * grad_scale

    return result, token_grad, total(level_parts, 1), total(in_parts, 0), total(out_parts, 0)


def solution(mesh):
    sizes = (mesh.shape["dp"], mesh.shape["hidden"])
    in_specs = (
        P("dp", "hidden"),
        P("dp", "hidden"),
        P("hidden", None),
        P(None, "hidden", None, None, None),
        P("hidden", None),
        P(),
    )
    out_specs = (
        P("dp", "hidden"),
        P("dp", "hidden"),
        P(None, "hidden", None, "dp", None),
        P(("hidden", "dp"), None),
        P(("hidden", "dp"), None),
    )
    return jax.shard_map(
        functools.partial(local, sizes), mesh=mesh, in_specs=in_specs, out_specs=out_specs, check_vma=False
    )
```

```python
import functools
import math

import jax
import jax.numpy as jnp
from jax import lax
from jax.experimental import pallas as pl
from jax.experimental.pallas import tpu as pltpu
from jax.sharding import PartitionSpec as P

WIDE = jnp.float32
NARROW = jnp.bfloat16
MESH = pl.DeviceIdType.MESH
LANES = 128
SUB = 8
GROUP = (4, 12, 3, 3, 4, 12, 4)
WINDOW = (8, 1, 1)


def chunk_rows(tokens):
    return (64,) * (tokens // 64)


def dot(a, b, dims):
    return lax.dot_general(a, b, (dims, ((), ())), preferred_element_type=WIDE)


def nn(a, b):
    return dot(a, b, ((1,), (0,)))


def nt(a, b):
    return dot(a, b, ((1,), (1,)))


def tn(a, b):
    return dot(a, b, ((0,), (0,)))


def gelu_pair(v):
    c = math.sqrt(2.0 / math.pi)
    square = v * v
    t = jnp.tanh(c * v * (1.0 + 0.044715 * square))
    half = 0.5 * (1.0 + t)
    slope = half + 0.5 * v * (1.0 - t * t) * c * (1.0 + 3.0 * 0.044715 * square)
    return v * half, slope


def schedule(levels, chunks):
    steps = {}

    def add(step, wish, *needs):
        steps[step] = (wish, needs)

    for c in range(chunks):
        add(("start", 0, c), c)
        for k in range(levels):
            before = ("start", 0, c) if k == 0 else ("forward", k - 1, c)
            wish = c + 1.5 if k == 0 else 10 + 4 * c + 5 * (k - 1)
            add(("forward", k, c), wish, before)
        add(("output", 0, c), 11 + 4 * c + 5 * (levels - 2), ("forward", levels - 1, c))
    top = 100
    done = [("forward", levels - 1, c) for c in range(chunks)]
    add(("output_grad", 0, 0), top, *done, *[("output", 0, c) for c in range(chunks)])
    for k in reversed(range(levels)):
        made = [("forward", levels - 1, c) if k == levels - 1 else ("backward", k + 1, c) for c in range(chunks)]
        deep = levels - 1 - k
        add(("level_grad", k, 0), top + 2 * deep + 2 * chunks - 1.5 if deep else top + 0.5, *made)
        for c in range(chunks):
            needs = [made[c], ("output_grad", 0, 0)]
            if k + 2 <= levels:
                needs.append(("level_grad", k + 1, 0))
            add(("backward", k, c), top + 1 + 2 * c + 2.5 * deep, *needs)
    order = []
    left = dict(steps)
    while left:
        ready = [s for s, (_, needs) in left.items() if not any(n in left for n in needs)]
        pick = min(ready, key=lambda s: left[s][0])
        order.append(pick)
        del left[pick]
    return order


def layer(
    plan,
    order,
    inverse,
    tokens,
    cotangent,
    weight_in,
    level_weights,
    weight_out,
    out_hbm,
    token_grad_hbm,
    level_parts,
    in_parts,
    out_parts,
    *scratch,
):
    L, N, sizes, Dl, NB, total_features = plan
    C, T = len(sizes), sum(sizes)
    begins = [sum(sizes[:c]) for c in range(C)]
    scratch = list(scratch)

    def take(count):
        taken = scratch[:count]
        del scratch[:count]
        return taken

    U = [take(C) for _ in range(L)]
    R = [take(C) for _ in range(L)]
    S = [take(C) for _ in range(2)]
    Tt = [take(C) for _ in range(2)]
    G = [take(C) for _ in range(2)]
    tok, cot, w_in, lw, w_out = take(5)
    recip, norm_t, xs, dn, acc, ost, lg = take(7)
    squares, squares_in, inner, inner_in = take(4)
    load_sem, fs, fr, bs, br, ps, pr, rs, rr, own_sem, credit, store_sem = take(12)
    act = S[1]

    hidden = lax.axis_index("hidden")
    dp = lax.axis_index("dp")
    partner = []
    for k in range(L):
        mask = 2**k
        bit = lax.rem(hidden // mask, 2)
        partner.append(hidden + mask - 2 * mask * bit)
    peers = [lax.rem(dp + off, N) for off in range(1, N)]

    barrier = pltpu.get_barrier_semaphore()
    for p in partner:
        pl.semaphore_signal(barrier, inc=1, device_id={"hidden": p}, device_id_type=MESH)
    for p in peers:
        pl.semaphore_signal(barrier, inc=1, device_id={"dp": p}, device_id_type=MESH)

    loads = [
        pltpu.make_async_copy(src, dst, load_sem.at[i])
        for i, (src, dst) in enumerate(
            ((tokens, tok), (weight_in, w_in), (level_weights, lw), (cotangent, cot), (weight_out, w_out))
        )
    ]
    for load in loads:
        load.start()
    loaded = set()

    def need(*which):
        for i in which:
            if i not in loaded:
                loaded.add(i)
                loads[i].wait()

    def to_hidden(src, dst, send, recv, k):
        return pltpu.make_async_remote_copy(
            src_ref=src,
            dst_ref=dst,
            send_sem=send,
            recv_sem=recv,
            device_id={"hidden": partner[k]},
            device_id_type=MESH,
        )

    def forward_copy(k, c):
        return to_hidden(U[k][c], R[k][c], fs.at[k, c], fr.at[k, c], k)

    def backward_copy(k, c):
        way = (L - 1 - k) % 2
        return to_hidden(S[way][c], Tt[way][c], bs.at[k, c], br.at[k, c], k)

    queues = [[(way, c) for way in (forward_copy, backward_copy) for c in range(C)] for _ in range(L)]
    made, landed, sent = [set() for _ in range(L)], [0] * L, [0] * L

    def move_on(k):
        while sent[k] < 2 * C and queues[k][sent[k]] in made[k] and sent[k] - WINDOW[min(k, 2)] < landed[k]:
            way, c = queues[k][sent[k]]
            way(k, c).start()
            sent[k] += 1

    def send(k, way, c):
        made[k].add((way, c))
        move_on(k)

    def receive(k, way, c):
        assert queues[k][landed[k]] == (way, c) and sent[k] > landed[k]
        way(k, c).wait_recv()
        landed[k] += 1
        move_on(k)

    def sum_copy(i, k, mine, inbox):
        return to_hidden(mine.at[k], inbox.at[k], ps.at[i, k], pr.at[i, k], k)

    def to_dp(i, off, src, dst):
        return pltpu.make_async_remote_copy(
            src_ref=src,
            dst_ref=dst,
            send_sem=rs.at[i, off - 1],
            recv_sem=rr.at[i, off - 1],
            device_id={"dp": peers[off - 1]},
            device_id_type=MESH,
        )

    out_share, in_share = out_parts.shape[1], in_parts.shape[1]

    def level_copy(k, off):
        return to_dp(k, off, lg.at[k, peers[off - 1]], level_parts.at[k, off])

    def in_rows(at):
        return pl.ds(pl.multiple_of(at * in_share, 16), in_share)

    def out_rows(at):
        return pl.ds(pl.multiple_of(at * out_share, 16), out_share)

    def in_copy(off):
        return to_dp(L, off, w_in.at[in_rows(peers[off - 1])], in_parts.at[off])

    def out_copy(off):
        return to_dp(L + 1, off, w_out.at[out_rows(peers[off - 1])], out_parts.at[off])

    own_copies = [pltpu.make_async_copy(lg.at[k, dp], level_parts.at[k, 0], own_sem.at[k]) for k in range(L)]
    own_copies.append(pltpu.make_async_copy(w_in.at[in_rows(dp)], in_parts.at[0], own_sem.at[L]))
    own_copies.append(pltpu.make_async_copy(w_out.at[out_rows(dp)], out_parts.at[0], own_sem.at[L + 1]))

    def rows(c):
        return pl.ds(begins[c], sizes[c])

    tiles = [pl.ds(at, LANES) for at in range(0, T, LANES)]

    def as_row(column):
        return jnp.broadcast_to(column, (LANES, LANES)).T[:SUB]

    def as_column(row):
        return jnp.broadcast_to(row[:1], (LANES, LANES)).T

    def groups(most, body, count=NB):
        size = max(n for n in range(1, most + 1) if count % n == 0)

        def step(i, carry):
            body([size * i + b for b in range(size)])
            return carry

        lax.fori_loop(0, count // size, step, 0)

    def pairs(most, body):
        groups(most, body, NB // 2)

    def wide_columns(i, width):
        return pl.ds(pl.multiple_of(i * width, width), width)

    need(0)
    for tile in tiles:
        x = tok[tile, :].astype(WIDE)
        squares[0, :, tile] = as_row(jnp.sum(x * x, axis=1, keepdims=True))
    pl.semaphore_wait(barrier, L + N - 1)
    for k in range(L):
        copy = sum_copy(0, k, squares, squares_in)
        copy.start()
        copy.wait()
        squares[k + 1] = squares[k] + squares_in[k]
    for tile in tiles:
        mean = squares[L, :, tile] / total_features
        recip[tile, :] = as_column(lax.rsqrt(mean + 1e-06))

    def start(_, c):
        need(1)
        here = pl.ds(0, sizes[c])
        xs[here, :] = (tok[rows(c), :].astype(WIDE) * recip[rows(c), :1]).astype(NARROW)

        def body(these):
            made = [nn(xs[here, :], w_in[:, wide_columns(i, 256)]).astype(NARROW) for i in these]
            for i, wide in zip(these, made):
                U[0][c][2 * i] = wide[:, :128]
                U[0][c][2 * i + 1] = wide[:, 128:]

        pairs(GROUP[0], body)
        send(0, forward_copy, c)

    def mixed(k, c, j):
        both = jnp.concatenate([U[k][c][j], R[k][c][order[k, j]]], axis=1)
        return nn(both, lw[k, j].reshape(256, 128)).astype(NARROW)

    def forward(k, c):
        need(2)
        receive(k, forward_copy, c)
        if k < L - 1:

            def body(these):
                made = [mixed(k, c, j) for j in these]
                for j, value in zip(these, made):
                    U[k + 1][c][j] = value

            groups(GROUP[1], body)
            send(k + 1, forward_copy, c)
            return
        need(3, 4)

        def body(these):
            blocks = [(n, b, 2 * i + b) for n, i in enumerate(these) for b in range(2)]
            tops = [mixed(k, c, j) for _, _, j in blocks]
            d_act = [nt(cot[rows(c), :], w_out[wide_columns(i, 256), :]) for i in these]
            values, grads = [], []
            for (n, b, _), top in zip(blocks, tops):
                value, slope = gelu_pair(top.astype(WIDE))
                values.append(value.astype(NARROW))
                grads.append((d_act[n][:, b * 128 : (b + 1) * 128] * slope).astype(NARROW))
            going = [nt(g, lw[k, j, 1]).astype(NARROW) for g, (_, _, j) in zip(grads, blocks)]
            for (_, _, j), value, g, s in zip(blocks, values, grads, going):
                act[c][j] = value
                G[0][c][j] = g
                S[0][c][j] = s

        pairs(GROUP[2], body)
        send(k, backward_copy, c)

    def output(_, c):
        here = pl.ds(0, sizes[c])
        acc[here, :] = jnp.zeros((sizes[c], Dl), WIDE)

        def step(q, carry):
            wide = jnp.concatenate([act[c][4 * q + b] for b in range(4)], axis=1)
            acc[here, :] += nn(wide, w_out[wide_columns(q, 512), :])
            return carry

        lax.fori_loop(0, NB // 4, step, 0)
        ost[rows(c), :] = acc[here, :].astype(NARROW)

    def all_rows(ref, j):
        return jnp.concatenate([ref[c][j] for c in range(C)], axis=0)

    def all_pair(ref, i):
        return jnp.concatenate([all_rows(ref, 2 * i), all_rows(ref, 2 * i + 1)], axis=1)

    out_store = pltpu.make_async_copy(ost, out_hbm, store_sem.at[0])
    token_store = pltpu.make_async_copy(tok, token_grad_hbm, store_sem.at[1])

    def output_grad(_, __):
        out_store.start()
        for tile in tiles:
            x = (tok[tile, :].astype(WIDE) * recip[tile, :1]).astype(NARROW)
            norm_t[:, tile] = x.astype(WIDE).T.astype(NARROW)

        def body(these):
            made = [tn(all_pair(act, i), cot[...]).astype(NARROW) for i in these]
            for i, value in zip(these, made):
                w_out[wide_columns(i, 256), :] = value

        pairs(GROUP[3], body)
        for off in range(1, N):
            out_copy(off).start()
        own_copies[L + 1].start()

    def level_grad(k, _):
        share = 128 // N

        def one(j):
            theirs = jnp.concatenate([R[k][c][order[k, j]] for c in range(C)], axis=0)
            both = jnp.concatenate([all_rows(U[k], j), theirs], axis=1)
            return tn(both, all_rows(G[(L - 1 - k) % 2], j)).astype(NARROW)

        def body(these):
            made = [one(j) for j in these]
            for j, value in zip(these, made):
                for r in range(N):
                    for b in range(2):
                        lg[k, r, j, b] = value[b * 128 + r * share : b * 128 + (r + 1) * share]

        groups(GROUP[4], body)
        for off in range(1, N):
            level_copy(k, off).start()
        own_copies[k].start()

    def backward(k, c):
        receive(k, backward_copy, c)
        if 0 < k < L - 1:
            backward_copy(k + 1, c).wait_send()
        upper, lower = G[(L - 1 - k) % 2], G[(L - k) % 2]
        came = Tt[(L - 1 - k) % 2][c]
        going = S[(L - k) % 2]

        def body(these):
            own = [nt(upper[c][j], lw[k, j, 0]) for j in these]
            grads = [(o + came[inverse[k, j]].astype(WIDE)).astype(NARROW) for o, j in zip(own, these)]
            leave = [nt(g, lw[k - 1, j, 1]).astype(NARROW) for g, j in zip(grads, these)] if k > 0 else []
            for j, g in zip(these, grads):
                lower[c][j] = g
            for j, value in zip(these, leave):
                going[c][j] = value

        groups(GROUP[5], body)
        if k >= 2:
            pl.semaphore_signal(
                credit.at[k - 2, c], inc=1, device_id={"hidden": partner[k - 2]}, device_id_type=MESH
            )
        if k > 0:
            if k - 1 <= L - 3:
                pl.semaphore_wait(credit.at[k - 1, c], 1)
            send(k - 1, backward_copy, c)
            return
        dn[rows(c), :] = jnp.zeros((sizes[c], Dl), WIDE)

        def step(q, carry):
            wide = jnp.concatenate([lower[c][4 * q + b] for b in range(4)], axis=1)
            dn[rows(c), :] += nt(wide, w_in[:, wide_columns(q, 512)])
            return carry

        lax.fori_loop(0, NB // 4, step, 0)
        for tile in tiles:
            if begins[c] < tile.start + LANES <= begins[c] + sizes[c]:
                dots = jnp.sum(dn[tile, :] * tok[tile, :].astype(WIDE), axis=1, keepdims=True)
                inner[0, :, tile] = as_row(dots)

    doing = dict(
        start=start,
        forward=forward,
        output=output,
        output_grad=output_grad,
        level_grad=level_grad,
        backward=backward,
    )
    for name, k, c in schedule(L, C):
        doing[name](k, c)

    first = G[L % 2]

    def in_grad(at):
        def body(these):
            made = [nn(norm_t[in_rows(at), :], all_pair(first, i)).astype(NARROW) for i in these]
            for i, value in zip(these, made):
                w_in[in_rows(at), wide_columns(i, 256)] = value

        pairs(GROUP[6], body)

    sum_copy(1, 0, inner, inner_in).start()
    for off in range(1, max(N, L) + 1):
        if off <= N:
            in_grad(peers[off - 1] if off < N else dp)
            (in_copy(off) if off < N else own_copies[L]).start()
        hop = off - 1
        if hop < L:
            sum_copy(1, hop, inner, inner_in).wait()
            inner[hop + 1] = inner[hop] + inner_in[hop]
            if hop + 1 < L:
                sum_copy(1, hop + 1, inner, inner_in).start()
    for tile in tiles:
        mean = as_column(inner[L, :, tile] / total_features)[:, :1]
        scale = recip[tile, :1]
        cube = scale * scale * scale
        wide = tok[tile, :].astype(WIDE)
        tok[tile, :] = (scale * dn[tile, :] - wide * (cube * mean)).astype(NARROW)
    token_store.start()

    for k in range(L):
        for c in range(C):
            forward_copy(k, c).wait_send()
            if k < 2:
                backward_copy(k, c).wait_send()
    for off in range(1, N):
        for k in range(L):
            level_copy(k, off).wait()
        out_copy(off).wait()
        in_copy(off).wait()
    for copy in own_copies:
        copy.wait()
    out_store.wait()
    token_store.wait()


def local(sizes, tokens, cotangent, weight_in, level_weights, weight_out, block_order):
    N, H = sizes
    T, Dl = tokens.shape
    L, NB = block_order.shape
    F = weight_in.shape[1]
    BLK = level_weights.shape[-1]
    chunks = chunk_rows(T)
    C, most = len(chunks), max(chunks)
    grad_scale = 1.0 / math.sqrt(T * N)
    seats = jnp.arange(NB, dtype=jnp.int32)
    inverse = jnp.sum(
        jnp.where(block_order[:, :, None] == seats[None, None, :], seats[None, :, None], 0), axis=1, dtype=jnp.int32
    )
    scratch = [pltpu.VMEM((NB, rows, BLK), NARROW) for rows in chunks] * (2 * L + 6)
    scratch += [
        pltpu.VMEM(a.shape, a.dtype) for a in (tokens, cotangent, weight_in, level_weights, weight_out)
    ]
    scratch += [
        pltpu.VMEM((T, LANES), WIDE),
        pltpu.VMEM((Dl, T), NARROW),
        pltpu.VMEM((most, Dl), NARROW),
        pltpu.VMEM((T, Dl), WIDE),
        pltpu.VMEM((most, Dl), WIDE),
        pltpu.VMEM((T, Dl), NARROW),
        pltpu.VMEM((L, N, NB, 2, BLK // N, BLK), NARROW),
    ]
    scratch += [pltpu.VMEM((count, SUB, T), WIDE) for count in (L + 1, L, L + 1, L)]
    dma = pltpu.SemaphoreType.DMA
    scratch += [dma((5,))] + [dma((L, C))] * 4 + [dma((2, L))] * 2 + [dma((L + 2, N - 1))] * 2 + [dma((L + 2,))]
    scratch += [pltpu.SemaphoreType.REGULAR((max(L - 2, 1), C)), dma((2,))]
    outs = (
        jax.ShapeDtypeStruct((T, Dl), NARROW),
        jax.ShapeDtypeStruct((T, Dl), NARROW),
        jax.ShapeDtypeStruct((L, N, NB, 2, BLK // N, BLK), NARROW),
        jax.ShapeDtypeStruct((N, Dl // N, F), NARROW),
        jax.ShapeDtypeStruct((N, F // N, Dl), NARROW),
    )
    plan = (L, N, chunks, Dl, NB, Dl * H)
    result, token_grad, level_parts, in_parts, out_parts = pl.pallas_call(
        functools.partial(layer, plan),
        out_shape=outs,
        in_specs=[pl.BlockSpec(memory_space=pltpu.SMEM)] * 2 + [pl.BlockSpec(memory_space=pl.ANY)] * 5,
        out_specs=[pl.BlockSpec(memory_space=pl.ANY)] * 5,
        scratch_shapes=scratch,
        compiler_params=pltpu.CompilerParams(
            collective_id=0, has_side_effects=True, vmem_limit_bytes=63 * 2**20
        ),
        cost_estimate=pl.CostEstimate(flops=18 * T * Dl * F, bytes_accessed=30 * 2**20, transcendentals=T * F),
    )(block_order, inverse, tokens, cotangent, weight_in, level_weights, weight_out)

    def total(parts, axis):
        split = [lax.index_in_dim(parts, i, axis, keepdims=False) for i in range(N)]
        return functools.reduce(jnp.add, [s.astype(WIDE) for s in split]) * grad_scale

    return result, token_grad, total(level_parts, 1), total(in_parts, 0), total(out_parts, 0)


def solution(mesh):
    sizes = (mesh.shape["dp"], mesh.shape["hidden"])
    in_specs = (
        P("dp", "hidden"),
        P("dp", "hidden"),
        P("hidden", None),
        P(None, "hidden", None, None, None),
        P("hidden", None),
        P(),
    )
    out_specs = (
        P("dp", "hidden"),
        P("dp", "hidden"),
        P(None, "hidden", None, "dp", None),
        P(("hidden", "dp"), None),
        P(("hidden", "dp"), None),
    )
    return jax.shard_map(
        functools.partial(local, sizes), mesh=mesh, in_specs=in_specs, out_specs=out_specs, check_vma=False
    )
```

```python
import functools
import math

import jax
import jax.numpy as jnp
from jax import lax
from jax.experimental import pallas as pl
from jax.experimental.pallas import tpu as pltpu
from jax.sharding import PartitionSpec as P

WIDE = jnp.float32
NARROW = jnp.bfloat16
MESH = pl.DeviceIdType.MESH
LANES = 128
SUB = 8
GROUP = (4, 12, 3, 3, 4, 12, 4)
WINDOW = (8, 1, 1)


def chunk_rows(tokens):
    return (64,) * (tokens // 64)


def dot(a, b, dims):
    return lax.dot_general(a, b, (dims, ((), ())), preferred_element_type=WIDE)


def nn(a, b):
    return dot(a, b, ((1,), (0,)))


def nt(a, b):
    return dot(a, b, ((1,), (1,)))


def tn(a, b):
    return dot(a, b, ((0,), (0,)))


def gelu_pair(v):
    c = math.sqrt(2.0 / math.pi)
    square = v * v
    t = jnp.tanh(c * v * (1.0 + 0.044715 * square))
    half = 0.5 * (1.0 + t)
    slope = half + 0.5 * v * (1.0 - t * t) * c * (1.0 + 3.0 * 0.044715 * square)
    return v * half, slope


def schedule(levels, chunks):
    steps = {}

    def add(step, wish, *needs):
        steps[step] = (wish, needs)

    for c in range(chunks):
        add(("start", 0, c), c)
        for k in range(levels):
            before = ("start", 0, c) if k == 0 else ("forward", k - 1, c)
            wish = c + 1.5 if k == 0 else 10 + 4 * c + 5 * (k - 1)
            add(("forward", k, c), wish, before)
        add(("output", 0, c), 11 + 4 * c + 5 * (levels - 2), ("forward", levels - 1, c))
    top = 100
    done = [("forward", levels - 1, c) for c in range(chunks)]
    add(("output_grad", 0, 0), top, *done, *[("output", 0, c) for c in range(chunks)])
    for k in reversed(range(levels)):
        made = [("forward", levels - 1, c) if k == levels - 1 else ("backward", k + 1, c) for c in range(chunks)]
        deep = levels - 1 - k
        add(("level_grad", k, 0), top + 2 * deep + 2 * chunks - 1.5 if deep else top + 0.5, *made)
        for c in range(chunks):
            needs = [made[c], ("output_grad", 0, 0)]
            if k + 2 <= levels:
                needs.append(("level_grad", k + 1, 0))
            add(("backward", k, c), top + 1 + 2 * c + 2.5 * deep, *needs)
    order = []
    left = dict(steps)
    while left:
        ready = [s for s, (_, needs) in left.items() if not any(n in left for n in needs)]
        pick = min(ready, key=lambda s: left[s][0])
        order.append(pick)
        del left[pick]
    return order


def layer(
    plan,
    order,
    inverse,
    tokens,
    cotangent,
    weight_in,
    level_weights,
    weight_out,
    out_hbm,
    token_grad_hbm,
    level_parts,
    in_parts,
    out_parts,
    *scratch,
):
    L, N, sizes, Dl, NB, total_features = plan
    C, T = len(sizes), sum(sizes)
    begins = [sum(sizes[:c]) for c in range(C)]
    scratch = list(scratch)

    def take(count):
        taken = scratch[:count]
        del scratch[:count]
        return taken

    U = [take(C) for _ in range(L)]
    R = [take(C) for _ in range(L)]
    S = [take(C) for _ in range(2)]
    Tt = [take(C) for _ in range(2)]
    G = [take(C) for _ in range(2)]
    tok, cot, w_in, lw, w_out = take(5)
    recip, norm_t, xs, dn, ost, lg = take(6)
    squares, squares_in, inner, inner_in = take(4)
    arrived = take(2)
    load_sem, fs, fr, bs, br, ps, pr, rs, rr, hs, hr, own_sem, credit, store_sem = take(14)
    act = S[1]
    out_stores = []

    hidden = lax.axis_index("hidden")
    dp = lax.axis_index("dp")
    partner = []
    for k in range(L):
        mask = 2**k
        bit = lax.rem(hidden // mask, 2)
        partner.append(hidden + mask - 2 * mask * bit)
    peers = [lax.rem(dp + off, N) for off in range(1, N)]

    barrier = pltpu.get_barrier_semaphore()
    for p in partner:
        pl.semaphore_signal(barrier, inc=1, device_id={"hidden": p}, device_id_type=MESH)
    for p in peers:
        pl.semaphore_signal(barrier, inc=1, device_id={"dp": p}, device_id_type=MESH)

    loads = [
        pltpu.make_async_copy(src, dst, load_sem.at[i])
        for i, (src, dst) in enumerate(
            ((tokens, tok), (weight_in, w_in), (level_weights, lw), (cotangent, cot), (weight_out, w_out))
        )
    ]
    for load in loads:
        load.start()
    loaded = set()

    def need(*which):
        for i in which:
            if i not in loaded:
                loaded.add(i)
                loads[i].wait()

    def to_hidden(src, dst, send, recv, k):
        return pltpu.make_async_remote_copy(
            src_ref=src,
            dst_ref=dst,
            send_sem=send,
            recv_sem=recv,
            device_id={"hidden": partner[k]},
            device_id_type=MESH,
        )

    def forward_copy(k, c):
        return to_hidden(U[k][c], R[k][c], fs.at[k, c], fr.at[k, c], k)

    def backward_copy(k, c):
        way = (L - 1 - k) % 2
        return to_hidden(S[way][c], Tt[way][c], bs.at[k, c], br.at[k, c], k)

    queues = [[(way, c) for way in (forward_copy, backward_copy) for c in range(C)] for _ in range(L)]
    made, landed, sent = [set() for _ in range(L)], [0] * L, [0] * L

    def move_on(k):
        while sent[k] < 2 * C and queues[k][sent[k]] in made[k] and sent[k] - WINDOW[min(k, 2)] < landed[k]:
            way, c = queues[k][sent[k]]
            way(k, c).start()
            sent[k] += 1

    def send(k, way, c):
        made[k].add((way, c))
        move_on(k)

    def receive(k, way, c):
        assert queues[k][landed[k]] == (way, c) and sent[k] > landed[k]
        way(k, c).wait_recv()
        landed[k] += 1
        move_on(k)

    def sum_copy(i, k, mine, inbox):
        return to_hidden(mine.at[k], inbox.at[k], ps.at[i, k], pr.at[i, k], k)

    def to_dp(i, off, src, dst):
        return pltpu.make_async_remote_copy(
            src_ref=src,
            dst_ref=dst,
            send_sem=rs.at[i, off - 1],
            recv_sem=rr.at[i, off - 1],
            device_id={"dp": peers[off - 1]},
            device_id_type=MESH,
        )

    out_share, in_share = out_parts.shape[1], in_parts.shape[1]

    def level_copy(k, off):
        return to_dp(k, off, lg.at[k % 2, peers[off - 1]], level_parts.at[k, off])

    def in_rows(at):
        return pl.ds(pl.multiple_of(at * in_share, 16), in_share)

    def out_rows(at):
        return pl.ds(pl.multiple_of(at * out_share, 16), out_share)

    bits = N.bit_length() - 1
    own_bit = [lax.rem(dp // 2**b, 2) for b in range(bits)]
    half = NB // 4 * 256

    def shares(side, step):
        ways = list(range(bits)) if side == 0 else list(reversed(range(bits)))
        b, rest = ways[step], ways[step + 1 :]
        fixed = sum((own_bit[p] * 2**p for p in ways[:step]), 0)
        free = [0]
        for q in rest:
            free = free + [f + 2**q for f in free]
        give = [fixed + (1 - own_bit[b]) * 2**b + f for f in free]
        keep = [fixed + own_bit[b] * 2**b + f for f in free]
        return give, keep, dp + 2**b - 2 * 2**b * own_bit[b]

    def seat(step, i):
        return sum(N >> (p + 1) for p in range(step)) + i

    def side_columns(side):
        return pl.ds(side * half, half)

    def half_copy(side, step, i):
        give, _, other = shares(side, step)
        last = step == bits - 1
        return pltpu.make_async_remote_copy(
            src_ref=w_in.at[in_rows(give[i]), side_columns(side)],
            dst_ref=in_parts.at[1, :, side_columns(side)] if last else arrived[side].at[seat(step, i)],
            send_sem=hs.at[side, seat(step, i)],
            recv_sem=hr.at[side, seat(step, i)],
            device_id={"dp": other},
            device_id_type=MESH,
        )

    def out_copy(off):
        return to_dp(L, off, w_out.at[out_rows(peers[off - 1])], out_parts.at[off])

    own_copies = [pltpu.make_async_copy(lg.at[k % 2, dp], level_parts.at[k, 0], own_sem.at[k]) for k in range(L)]
    own_copies.append(pltpu.make_async_copy(w_in.at[in_rows(dp)], in_parts.at[0], own_sem.at[L]))
    own_copies.append(pltpu.make_async_copy(w_out.at[out_rows(dp)], out_parts.at[0], own_sem.at[L + 1]))

    def rows(c):
        return pl.ds(begins[c], sizes[c])

    tiles = [pl.ds(at, LANES) for at in range(0, T, LANES)]

    def as_row(column):
        return jnp.broadcast_to(column, (LANES, LANES)).T[:SUB]

    def as_column(row):
        return jnp.broadcast_to(row[:1], (LANES, LANES)).T

    def groups(most, body, count=NB):
        size = max(n for n in range(1, most + 1) if count % n == 0)

        def step(i, carry):
            body([size * i + b for b in range(size)])
            return carry

        lax.fori_loop(0, count // size, step, 0)

    def pairs(most, body):
        groups(most, body, NB // 2)

    def wide_columns(i, width):
        return pl.ds(pl.multiple_of(i * width, width), width)

    need(0)
    for tile in tiles:
        x = tok[tile, :].astype(WIDE)
        squares[0, :, tile] = as_row(jnp.sum(x * x, axis=1, keepdims=True))
    pl.semaphore_wait(barrier, L + N - 1)
    for k in range(L):
        copy = sum_copy(0, k, squares, squares_in)
        copy.start()
        copy.wait()
        squares[k + 1] = squares[k] + squares_in[k]
    for tile in tiles:
        mean = squares[L, :, tile] / total_features
        recip[tile, :] = as_column(lax.rsqrt(mean + 1e-06))

    def start(_, c):
        need(1)
        here = pl.ds(0, sizes[c])
        xs[here, :] = (tok[rows(c), :].astype(WIDE) * recip[rows(c), :1]).astype(NARROW)

        def body(these):
            made = [nn(xs[here, :], w_in[:, wide_columns(i, 256)]).astype(NARROW) for i in these]
            for i, wide in zip(these, made):
                U[0][c][2 * i] = wide[:, :128]
                U[0][c][2 * i + 1] = wide[:, 128:]

        pairs(GROUP[0], body)
        send(0, forward_copy, c)

    def mixed(k, c, j):
        both = jnp.concatenate([U[k][c][j], R[k][c][order[k, j]]], axis=1)
        return nn(both, lw[k, j].reshape(256, 128)).astype(NARROW)

    def forward(k, c):
        need(2)
        receive(k, forward_copy, c)
        if k < L - 1:

            def body(these):
                made = [mixed(k, c, j) for j in these]
                for j, value in zip(these, made):
                    U[k + 1][c][j] = value

            groups(GROUP[1], body)
            send(k + 1, forward_copy, c)
            return
        need(3, 4)

        def body(these):
            blocks = [(n, b, 2 * i + b) for n, i in enumerate(these) for b in range(2)]
            tops = [mixed(k, c, j) for _, _, j in blocks]
            d_act = [nt(cot[rows(c), :], w_out[wide_columns(i, 256), :]) for i in these]
            values, grads = [], []
            for (n, b, _), top in zip(blocks, tops):
                value, slope = gelu_pair(top.astype(WIDE))
                values.append(value.astype(NARROW))
                grads.append((d_act[n][:, b * 128 : (b + 1) * 128] * slope).astype(NARROW))
            going = [nt(g, lw[k, j, 1]).astype(NARROW) for g, (_, _, j) in zip(grads, blocks)]
            for (_, _, j), value, g, s in zip(blocks, values, grads, going):
                act[c][j] = value
                G[0][c][j] = g
                S[0][c][j] = s

        pairs(GROUP[2], body)
        send(k, backward_copy, c)

    def output(_, c):
        here = pl.ds(0, sizes[c])
        slot = len(out_stores) % 2
        if len(out_stores) >= 2:
            out_stores[-2].wait()
        dn[here, :] = jnp.zeros((sizes[c], Dl), WIDE)

        def step(q, carry):
            wide = jnp.concatenate([act[c][4 * q + b] for b in range(4)], axis=1)
            dn[here, :] += nn(wide, w_out[wide_columns(q, 512), :])
            return carry

        lax.fori_loop(0, NB // 4, step, 0)
        ost[slot, here, :] = dn[here, :].astype(NARROW)
        out_stores.append(pltpu.make_async_copy(ost.at[slot, here], out_hbm.at[rows(c)], store_sem.at[1 + slot]))
        out_stores[-1].start()

    def all_rows(ref, j):
        return jnp.concatenate([ref[c][j] for c in range(C)], axis=0)

    def all_pair(ref, i):
        return jnp.concatenate([all_rows(ref, 2 * i), all_rows(ref, 2 * i + 1)], axis=1)

    token_store = pltpu.make_async_copy(tok, token_grad_hbm, store_sem.at[0])

    def output_grad(_, __):
        for tile in tiles:
            x = (tok[tile, :].astype(WIDE) * recip[tile, :1]).astype(NARROW)
            norm_t[:, tile] = x.astype(WIDE).T.astype(NARROW)

        def body(these):
            made = [tn(all_pair(act, i), cot[...]).astype(NARROW) for i in these]
            for i, value in zip(these, made):
                w_out[wide_columns(i, 256), :] = value

        pairs(GROUP[3], body)
        for off in range(1, N):
            out_copy(off).start()
        own_copies[L + 1].start()

    def level_grad(k, _):
        share = 128 // N
        if k + 2 < L:
            for off in range(1, N):
                level_copy(k + 2, off).wait_send()
            own_copies[k + 2].wait()

        def one(j):
            theirs = jnp.concatenate([R[k][c][order[k, j]] for c in range(C)], axis=0)
            both = jnp.concatenate([all_rows(U[k], j), theirs], axis=1)
            return tn(both, all_rows(G[(L - 1 - k) % 2], j)).astype(NARROW)

        def body(these):
            made = [one(j) for j in these]
            for j, value in zip(these, made):
                for r in range(N):
                    for b in range(2):
                        lg[k % 2, r, j, b] = value[b * 128 + r * share : b * 128 + (r + 1) * share]

        groups(GROUP[4], body)
        for off in range(1, N):
            level_copy(k, off).start()
        own_copies[k].start()

    def backward(k, c):
        receive(k, backward_copy, c)
        if 0 < k < L - 1:
            backward_copy(k + 1, c).wait_send()
        upper, lower = G[(L - 1 - k) % 2], G[(L - k) % 2]
        came = Tt[(L - 1 - k) % 2][c]
        going = S[(L - k) % 2]

        def body(these):
            own = [nt(upper[c][j], lw[k, j, 0]) for j in these]
            grads = [(o + came[inverse[k, j]].astype(WIDE)).astype(NARROW) for o, j in zip(own, these)]
            leave = [nt(g, lw[k - 1, j, 1]).astype(NARROW) for g, j in zip(grads, these)] if k > 0 else []
            for j, g in zip(these, grads):
                lower[c][j] = g
            for j, value in zip(these, leave):
                going[c][j] = value

        groups(GROUP[5], body)
        if k >= 2:
            pl.semaphore_signal(
                credit.at[k - 2, c], inc=1, device_id={"hidden": partner[k - 2]}, device_id_type=MESH
            )
        if k > 0:
            if k - 1 <= L - 3:
                pl.semaphore_wait(credit.at[k - 1, c], 1)
            send(k - 1, backward_copy, c)
            return
        dn[rows(c), :] = jnp.zeros((sizes[c], Dl), WIDE)

        def step(q, carry):
            wide = jnp.concatenate([lower[c][4 * q + b] for b in range(4)], axis=1)
            dn[rows(c), :] += nt(wide, w_in[:, wide_columns(q, 512)])
            return carry

        lax.fori_loop(0, NB // 4, step, 0)
        for tile in tiles:
            if begins[c] < tile.start + LANES <= begins[c] + sizes[c]:
                dots = jnp.sum(dn[tile, :] * tok[tile, :].astype(WIDE), axis=1, keepdims=True)
                inner[0, :, tile] = as_row(dots)

    doing = dict(
        start=start,
        forward=forward,
        output=output,
        output_grad=output_grad,
        level_grad=level_grad,
        backward=backward,
    )
    for name, k, c in schedule(L, C):
        doing[name](k, c)

    first = G[L % 2]

    def in_grad(at, side):
        def body(these):
            these = [i + side * (NB // 4) for i in these]
            made = [nn(norm_t[in_rows(at), :], all_pair(first, i)).astype(NARROW) for i in these]
            for i, value in zip(these, made):
                w_in[in_rows(at), wide_columns(i, 256)] = value

        groups(GROUP[6], body, NB // 4)

    hops = iter(range(L))

    def hop():
        k = next(hops, None)
        if k is not None:
            sum_copy(1, k, inner, inner_in).wait()
            inner[k + 1] = inner[k] + inner_in[k]
            if k + 1 < L:
                sum_copy(1, k + 1, inner, inner_in).start()

    sum_copy(1, 0, inner, inner_in).start()
    for i in range(N // 2):
        for side in range(2):
            in_grad(shares(side, 0)[0][i], side)
            half_copy(side, 0, i).start()
        hop()
    for i in range(N // 2):
        for side in range(2):
            in_grad(shares(side, 0)[1][i], side)
        hop()
    for _ in range(L):
        hop()
    for tile in tiles:
        mean = as_column(inner[L, :, tile] / total_features)[:, :1]
        scale = recip[tile, :1]
        cube = scale * scale * scale
        wide = tok[tile, :].astype(WIDE)
        tok[tile, :] = (scale * dn[tile, :] - wide * (cube * mean)).astype(NARROW)
    token_store.start()
    for step in range(bits - 1):
        count = N >> (step + 1)
        for i in range(count):
            for side in range(2):
                half_copy(side, step, i).wait()
                rows_here = in_rows(shares(side, step)[1][i])
                columns = side_columns(side)
                more = arrived[side][seat(step, i)].astype(WIDE)
                w_in[rows_here, columns] = (w_in[rows_here, columns].astype(WIDE) + more).astype(NARROW)
        for i in range(count // 2):
            for side in range(2):
                half_copy(side, step + 1, i).start()
    own_copies[L].start()

    for k in range(L):
        for c in range(C):
            forward_copy(k, c).wait_send()
            if k < 2:
                backward_copy(k, c).wait_send()
    for off in range(1, N):
        for k in range(L):
            level_copy(k, off).wait_recv()
            if k < 2:
                level_copy(k, off).wait_send()
        out_copy(off).wait()
    for side in range(2):
        half_copy(side, bits - 1, 0).wait()
    for copy in own_copies[:2] + own_copies[L:]:
        copy.wait()
    for copy in out_stores[-2:]:
        copy.wait()
    token_store.wait()


def local(sizes, tokens, cotangent, weight_in, level_weights, weight_out, block_order):
    N, H = sizes
    T, Dl = tokens.shape
    L, NB = block_order.shape
    F = weight_in.shape[1]
    BLK = level_weights.shape[-1]
    chunks = chunk_rows(T)
    C, most = len(chunks), max(chunks)
    grad_scale = 1.0 / math.sqrt(T * N)
    seats = jnp.arange(NB, dtype=jnp.int32)
    inverse = jnp.sum(
        jnp.where(block_order[:, :, None] == seats[None, None, :], seats[None, :, None], 0), axis=1, dtype=jnp.int32
    )
    scratch = [pltpu.VMEM((NB, rows, BLK), NARROW) for rows in chunks] * (2 * L + 6)
    scratch += [
        pltpu.VMEM(a.shape, a.dtype) for a in (tokens, cotangent, weight_in, level_weights, weight_out)
    ]
    scratch += [
        pltpu.VMEM((T, LANES), WIDE),
        pltpu.VMEM((Dl, T), NARROW),
        pltpu.VMEM((most, Dl), NARROW),
        pltpu.VMEM((T, Dl), WIDE),
        pltpu.VMEM((2, most, Dl), NARROW),
        pltpu.VMEM((2, N, NB, 2, BLK // N, BLK), NARROW),
    ]
    scratch += [pltpu.VMEM((count, SUB, T), WIDE) for count in (L + 1, L, L + 1, L)]
    scratch += [pltpu.VMEM((max(N - 2, 1), Dl // N, F // 2), NARROW)] * 2
    dma = pltpu.SemaphoreType.DMA
    scratch += [dma((5,))] + [dma((L, C))] * 4 + [dma((2, L))] * 2 + [dma((L + 1, N - 1))] * 2 + [dma((2, N - 1))] * 2 + [dma((L + 2,))]
    scratch += [pltpu.SemaphoreType.REGULAR((max(L - 2, 1), C)), dma((3,))]
    outs = (
        jax.ShapeDtypeStruct((T, Dl), NARROW),
        jax.ShapeDtypeStruct((T, Dl), NARROW),
        jax.ShapeDtypeStruct((L, N, NB, 2, BLK // N, BLK), NARROW),
        jax.ShapeDtypeStruct((2, Dl // N, F), NARROW),
        jax.ShapeDtypeStruct((N, F // N, Dl), NARROW),
    )
    plan = (L, N, chunks, Dl, NB, Dl * H)
    result, token_grad, level_parts, in_parts, out_parts = pl.pallas_call(
        functools.partial(layer, plan),
        out_shape=outs,
        in_specs=[pl.BlockSpec(memory_space=pltpu.SMEM)] * 2 + [pl.BlockSpec(memory_space=pl.ANY)] * 5,
        out_specs=[pl.BlockSpec(memory_space=pl.ANY)] * 5,
        scratch_shapes=scratch,
        compiler_params=pltpu.CompilerParams(
            collective_id=0, has_side_effects=True, vmem_limit_bytes=63 * 2**20
        ),
        cost_estimate=pl.CostEstimate(flops=18 * T * Dl * F, bytes_accessed=30 * 2**20, transcendentals=T * F),
    )(block_order, inverse, tokens, cotangent, weight_in, level_weights, weight_out)

    def total(parts, axis):
        split = [lax.index_in_dim(parts, i, axis, keepdims=False) for i in range(parts.shape[axis])]
        return functools.reduce(jnp.add, [s.astype(WIDE) for s in split]) * grad_scale

    return result, token_grad, total(level_parts, 1), total(in_parts, 0), total(out_parts, 0)


def solution(mesh):
    sizes = (mesh.shape["dp"], mesh.shape["hidden"])
    in_specs = (
        P("dp", "hidden"),
        P("dp", "hidden"),
        P("hidden", None),
        P(None, "hidden", None, None, None),
        P("hidden", None),
        P(),
    )
    out_specs = (
        P("dp", "hidden"),
        P("dp", "hidden"),
        P(None, "hidden", None, "dp", None),
        P(("hidden", "dp"), None),
        P(("hidden", "dp"), None),
    )
    return jax.shard_map(
        functools.partial(local, sizes), mesh=mesh, in_specs=in_specs, out_specs=out_specs, check_vma=False
    )
```

```python
import functools
import math

import jax
import jax.numpy as jnp
from jax import lax
from jax.experimental import pallas as pl
from jax.experimental.pallas import tpu as pltpu
from jax.sharding import PartitionSpec as P

WIDE = jnp.float32
NARROW = jnp.bfloat16
MESH = pl.DeviceIdType.MESH
LANES = 128
SUB = 8
GROUP = (4, 12, 3, 3, 4, 12, 4)
WINDOW = (8, 1, 1)


def chunk_rows(tokens):
    return (64,) * (tokens // 64)


def dot(a, b, dims):
    return lax.dot_general(a, b, (dims, ((), ())), preferred_element_type=WIDE)


def nn(a, b):
    return dot(a, b, ((1,), (0,)))


def nt(a, b):
    return dot(a, b, ((1,), (1,)))


def tn(a, b):
    return dot(a, b, ((0,), (0,)))


def gelu_pair(v):
    c = math.sqrt(2.0 / math.pi)
    square = v * v
    t = jnp.tanh(c * v * (1.0 + 0.044715 * square))
    half = 0.5 * (1.0 + t)
    slope = half + 0.5 * v * (1.0 - t * t) * c * (1.0 + 3.0 * 0.044715 * square)
    return v * half, slope


def schedule(levels, chunks):
    steps = {}

    def add(step, wish, *needs):
        steps[step] = (wish, needs)

    for c in range(chunks):
        add(("start", 0, c), c)
        for k in range(levels):
            before = ("start", 0, c) if k == 0 else ("forward", k - 1, c)
            wish = c + 1.5 if k == 0 else 10 + 4 * c + 5 * (k - 1)
            add(("forward", k, c), wish, before)
        add(("output", 0, c), 11 + 4 * c + 5 * (levels - 2), ("forward", levels - 1, c))
    top = 100
    done = [("forward", levels - 1, c) for c in range(chunks)]
    add(("output_grad", 0, 0), top, *done, *[("output", 0, c) for c in range(chunks)])
    for k in reversed(range(levels)):
        made = [("forward", levels - 1, c) if k == levels - 1 else ("backward", k + 1, c) for c in range(chunks)]
        deep = levels - 1 - k
        add(("level_grad", k, 0), top + 2 * deep + 2 * chunks - 1.5 if deep else top + 0.5, *made)
        for c in range(chunks):
            needs = [made[c], ("output_grad", 0, 0)]
            if k + 2 <= levels:
                needs.append(("level_grad", k + 1 if k else levels - 1, 0))
            add(("backward", k, c), top + 1 + 2 * c + 2.5 * deep, *needs)
    order = []
    left = dict(steps)
    while left:
        ready = [s for s, (_, needs) in left.items() if not any(n in left for n in needs)]
        pick = min(ready, key=lambda s: left[s][0])
        order.append(pick)
        del left[pick]
    return order


def layer(
    plan,
    order,
    inverse,
    tokens,
    cotangent,
    weight_in,
    level_weights,
    weight_out,
    out_hbm,
    token_grad_hbm,
    level_parts,
    in_parts,
    out_parts,
    *scratch,
):
    L, N, sizes, Dl, NB, total_features = plan
    C, T = len(sizes), sum(sizes)
    begins = [sum(sizes[:c]) for c in range(C)]
    scratch = list(scratch)

    def take(count):
        taken = scratch[:count]
        del scratch[:count]
        return taken

    U = [take(C) for _ in range(L)]
    R = [take(C) for _ in range(L)]
    S = [take(C) for _ in range(2)]
    Tt = [take(C) for _ in range(2)]
    G = [take(C) for _ in range(2)]
    tok, cot, w_in, lw, w_out = take(5)
    recip, norm_t, xs, dn, ost, lg = take(6)
    squares, squares_in, inner, inner_in = take(4)
    arrived = take(2)
    load_sem, fs, fr, bs, br, ps, pr, rs, rr, hs, hr, own_sem, credit, store_sem = take(14)
    act = S[1]
    out_stores = []

    hidden = lax.axis_index("hidden")
    dp = lax.axis_index("dp")
    partner = []
    for k in range(L):
        mask = 2**k
        bit = lax.rem(hidden // mask, 2)
        partner.append(hidden + mask - 2 * mask * bit)
    peers = [lax.rem(dp + off, N) for off in range(1, N)]

    barrier = pltpu.get_barrier_semaphore()
    for p in partner:
        pl.semaphore_signal(barrier, inc=1, device_id={"hidden": p}, device_id_type=MESH)
    for p in peers:
        pl.semaphore_signal(barrier, inc=1, device_id={"dp": p}, device_id_type=MESH)

    loads = [
        pltpu.make_async_copy(src, dst, load_sem.at[i])
        for i, (src, dst) in enumerate(
            ((tokens, tok), (weight_in, w_in), (level_weights, lw), (cotangent, cot), (weight_out, w_out))
        )
    ]
    for load in loads:
        load.start()
    loaded = set()

    def need(*which):
        for i in which:
            if i not in loaded:
                loaded.add(i)
                loads[i].wait()

    def to_hidden(src, dst, send, recv, k):
        return pltpu.make_async_remote_copy(
            src_ref=src,
            dst_ref=dst,
            send_sem=send,
            recv_sem=recv,
            device_id={"hidden": partner[k]},
            device_id_type=MESH,
        )

    def forward_copy(k, c):
        return to_hidden(U[k][c], R[k][c], fs.at[k, c], fr.at[k, c], k)

    def backward_copy(k, c):
        way = (L - 1 - k) % 2
        return to_hidden(S[way][c], Tt[way][c], bs.at[k, c], br.at[k, c], k)

    queues = [[(way, c) for way in (forward_copy, backward_copy) for c in range(C)] for _ in range(L)]
    made, landed, sent = [set() for _ in range(L)], [0] * L, [0] * L

    def move_on(k):
        while sent[k] < 2 * C and queues[k][sent[k]] in made[k] and sent[k] - WINDOW[min(k, 2)] < landed[k]:
            way, c = queues[k][sent[k]]
            way(k, c).start()
            sent[k] += 1

    def send(k, way, c):
        made[k].add((way, c))
        move_on(k)

    def receive(k, way, c):
        assert queues[k][landed[k]] == (way, c) and sent[k] > landed[k]
        way(k, c).wait_recv()
        landed[k] += 1
        move_on(k)

    def sum_copy(i, k, mine, inbox):
        return to_hidden(mine.at[k], inbox.at[k], ps.at[i, k], pr.at[i, k], k)

    def to_dp(i, off, src, dst):
        return pltpu.make_async_remote_copy(
            src_ref=src,
            dst_ref=dst,
            send_sem=rs.at[i, off - 1],
            recv_sem=rr.at[i, off - 1],
            device_id={"dp": peers[off - 1]},
            device_id_type=MESH,
        )

    out_share, in_share = out_parts.shape[1], in_parts.shape[1]

    def level_copy(k, off):
        return to_dp(k, off, lg.at[k % 2, peers[off - 1]], level_parts.at[k, off])

    def in_rows(at):
        return pl.ds(pl.multiple_of(at * in_share, 16), in_share)

    def out_rows(at):
        return pl.ds(pl.multiple_of(at * out_share, 16), out_share)

    bits = N.bit_length() - 1
    own_bit = [lax.rem(dp // 2**b, 2) for b in range(bits)]
    half = NB // 4 * 256

    def shares(side, step):
        ways = list(range(bits)) if side == 0 else list(reversed(range(bits)))
        b, rest = ways[step], ways[step + 1 :]
        fixed = sum((own_bit[p] * 2**p for p in ways[:step]), 0)
        free = [0]
        for q in rest:
            free = free + [f + 2**q for f in free]
        give = [fixed + (1 - own_bit[b]) * 2**b + f for f in free]
        keep = [fixed + own_bit[b] * 2**b + f for f in free]
        return give, keep, dp + 2**b - 2 * 2**b * own_bit[b]

    def seat(step, i):
        return sum(N >> (p + 1) for p in range(step)) + i

    def side_columns(side):
        return pl.ds(side * half, half)

    def half_copy(side, step, i):
        give, _, other = shares(side, step)
        last = step == bits - 1
        return pltpu.make_async_remote_copy(
            src_ref=w_in.at[in_rows(give[i]), side_columns(side)],
            dst_ref=in_parts.at[1, :, side_columns(side)] if last else arrived[side].at[seat(step, i)],
            send_sem=hs.at[side, seat(step, i)],
            recv_sem=hr.at[side, seat(step, i)],
            device_id={"dp": other},
            device_id_type=MESH,
        )

    def out_copy(off):
        return to_dp(L, off, w_out.at[out_rows(peers[off - 1])], out_parts.at[off])

    own_copies = [pltpu.make_async_copy(lg.at[k % 2, dp], level_parts.at[k, 0], own_sem.at[k]) for k in range(L)]
    own_copies.append(pltpu.make_async_copy(w_in.at[in_rows(dp)], in_parts.at[0], own_sem.at[L]))
    own_copies.append(pltpu.make_async_copy(w_out.at[out_rows(dp)], out_parts.at[0], own_sem.at[L + 1]))

    def rows(c):
        return pl.ds(begins[c], sizes[c])

    tiles = [pl.ds(at, LANES) for at in range(0, T, LANES)]

    def as_row(column):
        return jnp.broadcast_to(column, (LANES, LANES)).T[:SUB]

    def as_column(row):
        return jnp.broadcast_to(row[:1], (LANES, LANES)).T

    def groups(most, body, count=NB):
        size = max(n for n in range(1, most + 1) if count % n == 0)

        def step(i, carry):
            body([size * i + b for b in range(size)])
            return carry

        lax.fori_loop(0, count // size, step, 0)

    def pairs(most, body):
        groups(most, body, NB // 2)

    def wide_columns(i, width):
        return pl.ds(pl.multiple_of(i * width, width), width)

    need(0)
    for tile in tiles:
        x = tok[tile, :].astype(WIDE)
        squares[0, :, tile] = as_row(jnp.sum(x * x, axis=1, keepdims=True))
    pl.semaphore_wait(barrier, L + N - 1)
    for k in range(L):
        copy = sum_copy(0, k, squares, squares_in)
        copy.start()
        copy.wait()
        squares[k + 1] = squares[k] + squares_in[k]
    for tile in tiles:
        mean = squares[L, :, tile] / total_features
        recip[tile, :] = as_column(lax.rsqrt(mean + 1e-06))

    def start(_, c):
        need(1)
        here = pl.ds(0, sizes[c])
        xs[here, :] = (tok[rows(c), :].astype(WIDE) * recip[rows(c), :1]).astype(NARROW)

        def body(these):
            made = [nn(xs[here, :], w_in[:, wide_columns(i, 256)]).astype(NARROW) for i in these]
            for i, wide in zip(these, made):
                U[0][c][2 * i] = wide[:, :128]
                U[0][c][2 * i + 1] = wide[:, 128:]

        pairs(GROUP[0], body)
        send(0, forward_copy, c)

    def mixed(k, c, j):
        both = jnp.concatenate([U[k][c][j], R[k][c][order[k, j]]], axis=1)
        return nn(both, lw[k, j].reshape(256, 128)).astype(NARROW)

    def forward(k, c):
        need(2)
        receive(k, forward_copy, c)
        if k < L - 1:

            def body(these):
                made = [mixed(k, c, j) for j in these]
                for j, value in zip(these, made):
                    U[k + 1][c][j] = value

            groups(GROUP[1], body)
            send(k + 1, forward_copy, c)
            return
        need(3, 4)

        def body(these):
            blocks = [(n, b, 2 * i + b) for n, i in enumerate(these) for b in range(2)]
            tops = [mixed(k, c, j) for _, _, j in blocks]
            d_act = [nt(cot[rows(c), :], w_out[wide_columns(i, 256), :]) for i in these]
            values, grads = [], []
            for (n, b, _), top in zip(blocks, tops):
                value, slope = gelu_pair(top.astype(WIDE))
                values.append(value.astype(NARROW))
                grads.append((d_act[n][:, b * 128 : (b + 1) * 128] * slope).astype(NARROW))
            going = [nt(g, lw[k, j, 1]).astype(NARROW) for g, (_, _, j) in zip(grads, blocks)]
            for (_, _, j), value, g, s in zip(blocks, values, grads, going):
                act[c][j] = value
                G[0][c][j] = g
                S[0][c][j] = s

        pairs(GROUP[2], body)
        send(k, backward_copy, c)

    def output(_, c):
        here = pl.ds(0, sizes[c])
        slot = len(out_stores) % 2
        if len(out_stores) >= 2:
            out_stores[-2].wait()
        dn[here, :] = jnp.zeros((sizes[c], Dl), WIDE)

        def step(q, carry):
            wide = jnp.concatenate([act[c][4 * q + b] for b in range(4)], axis=1)
            dn[here, :] += nn(wide, w_out[wide_columns(q, 512), :])
            return carry

        lax.fori_loop(0, NB // 4, step, 0)
        ost[slot, here, :] = dn[here, :].astype(NARROW)
        out_stores.append(pltpu.make_async_copy(ost.at[slot, here], out_hbm.at[rows(c)], store_sem.at[1 + slot]))
        out_stores[-1].start()

    def all_rows(ref, j):
        return jnp.concatenate([ref[c][j] for c in range(C)], axis=0)

    def all_pair(ref, i):
        return jnp.concatenate([all_rows(ref, 2 * i), all_rows(ref, 2 * i + 1)], axis=1)

    token_store = pltpu.make_async_copy(tok, token_grad_hbm, store_sem.at[0])

    def output_grad(_, __):
        for tile in tiles:
            x = (tok[tile, :].astype(WIDE) * recip[tile, :1]).astype(NARROW)
            norm_t[:, tile] = x.astype(WIDE).T.astype(NARROW)

        def body(these):
            made = [tn(all_pair(act, i), cot[...]).astype(NARROW) for i in these]
            for i, value in zip(these, made):
                w_out[wide_columns(i, 256), :] = value

        pairs(GROUP[3], body)
        for off in range(1, N):
            out_copy(off).start()
        own_copies[L + 1].start()

    def level_grad(k, _):
        share = 128 // N
        if k + 2 < L:
            for off in range(1, N):
                level_copy(k + 2, off).wait_send()
            own_copies[k + 2].wait()

        def one(j):
            theirs = jnp.concatenate([R[k][c][order[k, j]] for c in range(C)], axis=0)
            both = jnp.concatenate([all_rows(U[k], j), theirs], axis=1)
            return tn(both, all_rows(G[(L - 1 - k) % 2], j)).astype(NARROW)

        def body(these):
            made = [one(j) for j in these]
            for j, value in zip(these, made):
                for r in range(N):
                    for b in range(2):
                        lg[k % 2, r, j, b] = value[b * 128 + r * share : b * 128 + (r + 1) * share]

        groups(GROUP[4], body)
        for off in range(1, N):
            level_copy(k, off).start()
        own_copies[k].start()

    def backward(k, c):
        receive(k, backward_copy, c)
        if 0 < k < L - 1:
            backward_copy(k + 1, c).wait_send()
        upper, lower = G[(L - 1 - k) % 2], G[(L - k) % 2] if k else U[L - 1]
        if k == 0:
            forward_copy(L - 1, c).wait_send()
        came = Tt[(L - 1 - k) % 2][c]
        going = S[(L - k) % 2]

        def body(these):
            own = [nt(upper[c][j], lw[k, j, 0]) for j in these]
            grads = [(o + came[inverse[k, j]].astype(WIDE)).astype(NARROW) for o, j in zip(own, these)]
            leave = [nt(g, lw[k - 1, j, 1]).astype(NARROW) for g, j in zip(grads, these)] if k > 0 else []
            for j, g in zip(these, grads):
                lower[c][j] = g
            for j, value in zip(these, leave):
                going[c][j] = value

        groups(GROUP[5], body)
        if k >= 2:
            pl.semaphore_signal(
                credit.at[k - 2, c], inc=1, device_id={"hidden": partner[k - 2]}, device_id_type=MESH
            )
        if k > 0:
            if k - 1 <= L - 3:
                pl.semaphore_wait(credit.at[k - 1, c], 1)
            send(k - 1, backward_copy, c)
            return
        dn[rows(c), :] = jnp.zeros((sizes[c], Dl), WIDE)

        def step(q, carry):
            wide = jnp.concatenate([lower[c][4 * q + b] for b in range(4)], axis=1)
            dn[rows(c), :] += nt(wide, w_in[:, wide_columns(q, 512)])
            return carry

        lax.fori_loop(0, NB // 4, step, 0)
        for tile in tiles:
            if begins[c] < tile.start + LANES <= begins[c] + sizes[c]:
                dots = jnp.sum(dn[tile, :] * tok[tile, :].astype(WIDE), axis=1, keepdims=True)
                inner[0, :, tile] = as_row(dots)

    doing = dict(
        start=start,
        forward=forward,
        output=output,
        output_grad=output_grad,
        level_grad=level_grad,
        backward=backward,
    )
    for name, k, c in schedule(L, C):
        doing[name](k, c)

    first = U[L - 1]

    def in_grad(at, side):
        def body(these):
            these = [i + side * (NB // 4) for i in these]
            made = [nn(norm_t[in_rows(at), :], all_pair(first, i)).astype(NARROW) for i in these]
            for i, value in zip(these, made):
                w_in[in_rows(at), wide_columns(i, 256)] = value

        groups(GROUP[6], body, NB // 4)

    hops = iter(range(L))

    def hop():
        k = next(hops, None)
        if k is not None:
            sum_copy(1, k, inner, inner_in).wait()
            inner[k + 1] = inner[k] + inner_in[k]
            if k + 1 < L:
                sum_copy(1, k + 1, inner, inner_in).start()

    sum_copy(1, 0, inner, inner_in).start()
    for i in range(N // 2):
        for side in range(2):
            in_grad(shares(side, 0)[0][i], side)
            half_copy(side, 0, i).start()
        hop()
    for i in range(N // 2):
        for side in range(2):
            in_grad(shares(side, 0)[1][i], side)
        hop()
    for _ in range(L):
        hop()
    for tile in tiles:
        mean = as_column(inner[L, :, tile] / total_features)[:, :1]
        scale = recip[tile, :1]
        cube = scale * scale * scale
        wide = tok[tile, :].astype(WIDE)
        tok[tile, :] = (scale * dn[tile, :] - wide * (cube * mean)).astype(NARROW)
    token_store.start()
    for step in range(bits - 1):
        count = N >> (step + 1)
        for i in range(count):
            for side in range(2):
                half_copy(side, step, i).wait()
                rows_here = in_rows(shares(side, step)[1][i])
                columns = side_columns(side)
                more = arrived[side][seat(step, i)].astype(WIDE)
                w_in[rows_here, columns] = (w_in[rows_here, columns].astype(WIDE) + more).astype(NARROW)
        for i in range(count // 2):
            for side in range(2):
                half_copy(side, step + 1, i).start()
    own_copies[L].start()

    for k in range(L):
        for c in range(C):
            if k < L - 1:
                forward_copy(k, c).wait_send()
            if k < 2:
                backward_copy(k, c).wait_send()
    for off in range(1, N):
        for k in range(L):
            level_copy(k, off).wait_recv()
            if k < 2:
                level_copy(k, off).wait_send()
        out_copy(off).wait()
    for side in range(2):
        half_copy(side, bits - 1, 0).wait()
    for copy in own_copies[:2] + own_copies[L:]:
        copy.wait()
    for copy in out_stores[-2:]:
        copy.wait()
    token_store.wait()


def local(sizes, tokens, cotangent, weight_in, level_weights, weight_out, block_order):
    N, H = sizes
    T, Dl = tokens.shape
    L, NB = block_order.shape
    F = weight_in.shape[1]
    BLK = level_weights.shape[-1]
    chunks = chunk_rows(T)
    C, most = len(chunks), max(chunks)
    grad_scale = 1.0 / math.sqrt(T * N)
    seats = jnp.arange(NB, dtype=jnp.int32)
    inverse = jnp.sum(
        jnp.where(block_order[:, :, None] == seats[None, None, :], seats[None, :, None], 0), axis=1, dtype=jnp.int32
    )
    scratch = [pltpu.VMEM((NB, rows, BLK), NARROW) for rows in chunks] * (2 * L + 6)
    scratch += [
        pltpu.VMEM(a.shape, a.dtype) for a in (tokens, cotangent, weight_in, level_weights, weight_out)
    ]
    scratch += [
        pltpu.VMEM((T, LANES), WIDE),
        pltpu.VMEM((Dl, T), NARROW),
        pltpu.VMEM((most, Dl), NARROW),
        pltpu.VMEM((T, Dl), WIDE),
        pltpu.VMEM((2, most, Dl), NARROW),
        pltpu.VMEM((2, N, NB, 2, BLK // N, BLK), NARROW),
    ]
    scratch += [pltpu.VMEM((count, SUB, T), WIDE) for count in (L + 1, L, L + 1, L)]
    scratch += [pltpu.VMEM((max(N - 2, 1), Dl // N, F // 2), NARROW)] * 2
    dma = pltpu.SemaphoreType.DMA
    scratch += [dma((5,))] + [dma((L, C))] * 4 + [dma((2, L))] * 2 + [dma((L + 1, N - 1))] * 2 + [dma((2, N - 1))] * 2 + [dma((L + 2,))]
    scratch += [pltpu.SemaphoreType.REGULAR((max(L - 2, 1), C)), dma((3,))]
    outs = (
        jax.ShapeDtypeStruct((T, Dl), NARROW),
        jax.ShapeDtypeStruct((T, Dl), NARROW),
        jax.ShapeDtypeStruct((L, N, NB, 2, BLK // N, BLK), NARROW),
        jax.ShapeDtypeStruct((2, Dl // N, F), NARROW),
        jax.ShapeDtypeStruct((N, F // N, Dl), NARROW),
    )
    plan = (L, N, chunks, Dl, NB, Dl * H)
    result, token_grad, level_parts, in_parts, out_parts = pl.pallas_call(
        functools.partial(layer, plan),
        out_shape=outs,
        in_specs=[pl.BlockSpec(memory_space=pltpu.SMEM)] * 2 + [pl.BlockSpec(memory_space=pl.ANY)] * 5,
        out_specs=[pl.BlockSpec(memory_space=pl.ANY)] * 5,
        scratch_shapes=scratch,
        compiler_params=pltpu.CompilerParams(
            collective_id=0, has_side_effects=True, vmem_limit_bytes=63 * 2**20
        ),
        cost_estimate=pl.CostEstimate(flops=18 * T * Dl * F, bytes_accessed=30 * 2**20, transcendentals=T * F),
    )(block_order, inverse, tokens, cotangent, weight_in, level_weights, weight_out)

    def total(parts, axis):
        split = [lax.index_in_dim(parts, i, axis, keepdims=False) for i in range(parts.shape[axis])]
        return functools.reduce(jnp.add, [s.astype(WIDE) for s in split]) * grad_scale

    return result, token_grad, total(level_parts, 1), total(in_parts, 0), total(out_parts, 0)


def solution(mesh):
    sizes = (mesh.shape["dp"], mesh.shape["hidden"])
    in_specs = (
        P("dp", "hidden"),
        P("dp", "hidden"),
        P("hidden", None),
        P(None, "hidden", None, None, None),
        P("hidden", None),
        P(),
    )
    out_specs = (
        P("dp", "hidden"),
        P("dp", "hidden"),
        P(None, "hidden", None, "dp", None),
        P(("hidden", "dp"), None),
        P(("hidden", "dp"), None),
    )
    return jax.shard_map(
        functools.partial(local, sizes), mesh=mesh, in_specs=in_specs, out_specs=out_specs, check_vma=False
    )
```

```python
import functools
import math

import jax
import jax.numpy as jnp
from jax import lax
from jax.experimental import pallas as pl
from jax.experimental.pallas import tpu as pltpu
from jax.sharding import PartitionSpec as P

WIDE = jnp.float32
NARROW = jnp.bfloat16
MESH = pl.DeviceIdType.MESH
LANES = 128
SUB = 8
GROUP = (4, 12, 3, 3, 4, 12, 4)
WINDOW = (8, 1, 1)


def chunk_rows(tokens):
    return (64,) * (tokens // 64)


def dot(a, b, dims):
    return lax.dot_general(a, b, (dims, ((), ())), preferred_element_type=WIDE)


def nn(a, b):
    return dot(a, b, ((1,), (0,)))


def nt(a, b):
    return dot(a, b, ((1,), (1,)))


def tn(a, b):
    return dot(a, b, ((0,), (0,)))


def gelu_pair(v):
    c = math.sqrt(2.0 / math.pi)
    square = v * v
    t = jnp.tanh(c * v * (1.0 + 0.044715 * square))
    half = 0.5 * (1.0 + t)
    slope = half + 0.5 * v * (1.0 - t * t) * c * (1.0 + 3.0 * 0.044715 * square)
    return v * half, slope


def schedule(levels, chunks):
    steps = {}

    def add(step, wish, *needs):
        steps[step] = (wish, needs)

    for c in range(chunks):
        add(("start", 0, c), c)
        for k in range(levels):
            before = ("start", 0, c) if k == 0 else ("forward", k - 1, c)
            wish = c + 1.5 if k == 0 else 10 + 4 * c + 5 * (k - 1)
            add(("forward", k, c), wish, before)
        add(("output", 0, c), 11 + 4 * c + 5 * (levels - 2), ("forward", levels - 1, c))
    top = 100
    done = [("forward", levels - 1, c) for c in range(chunks)]
    add(("output_grad", 0, 0), top, *done, *[("output", 0, c) for c in range(chunks)])
    for k in reversed(range(levels)):
        made = [("forward", levels - 1, c) if k == levels - 1 else ("backward", k + 1, c) for c in range(chunks)]
        deep = levels - 1 - k
        add(("level_grad", k, 0), top + 2 * deep + 2 * chunks - 1.5 if deep else top + 0.5, *made)
        for c in range(chunks):
            needs = [made[c], ("output_grad", 0, 0)]
            if k + 2 <= levels:
                needs.append(("level_grad", k + 1 if k else levels - 1, 0))
            add(("backward", k, c), top + 1 + 2 * c + 2.5 * deep, *needs)
    order = []
    left = dict(steps)
    while left:
        ready = [s for s, (_, needs) in left.items() if not any(n in left for n in needs)]
        pick = min(ready, key=lambda s: left[s][0])
        order.append(pick)
        del left[pick]
    return order


def layer(
    plan,
    order,
    inverse,
    tokens,
    cotangent,
    weight_in,
    level_weights,
    weight_out,
    out_hbm,
    token_grad_hbm,
    level_parts,
    in_parts,
    out_parts,
    *scratch,
):
    L, N, sizes, Dl, NB, total_features = plan
    C, T = len(sizes), sum(sizes)
    begins = [sum(sizes[:c]) for c in range(C)]
    scratch = list(scratch)

    def take(count):
        taken = scratch[:count]
        del scratch[:count]
        return taken

    U = [take(C) for _ in range(L)]
    R = [take(C) for _ in range(L)]
    S = [take(C) for _ in range(2)]
    Tt = [take(C) for _ in range(2)]
    G = [take(C) for _ in range(2)]
    tok, cot, w_in, lw, w_out = take(5)
    recip, norm_t, xs, dn, ost, lg = take(6)
    squares, squares_in, inner, inner_in = take(4)
    arrived = take(2)
    load_sem, fs, fr, bs, br, ps, pr, rs, rr, hs, hr, own_sem, credit, store_sem = take(14)
    act = S[1]
    out_stores = []

    hidden = lax.axis_index("hidden")
    dp = lax.axis_index("dp")
    partner = []
    for k in range(L):
        mask = 2**k
        bit = lax.rem(hidden // mask, 2)
        partner.append(hidden + mask - 2 * mask * bit)
    peers = [lax.rem(dp + off, N) for off in range(1, N)]

    barrier = pltpu.get_barrier_semaphore()
    for p in partner:
        pl.semaphore_signal(barrier, inc=1, device_id={"hidden": p}, device_id_type=MESH)
    for p in peers:
        pl.semaphore_signal(barrier, inc=1, device_id={"dp": p}, device_id_type=MESH)

    loads = [
        pltpu.make_async_copy(src, dst, load_sem.at[i])
        for i, (src, dst) in enumerate(
            ((tokens, tok), (weight_in, w_in), (level_weights, lw), (cotangent, cot), (weight_out, w_out))
        )
    ]
    for load in loads:
        load.start()
    loaded = set()

    def need(*which):
        for i in which:
            if i not in loaded:
                loaded.add(i)
                loads[i].wait()

    def to_hidden(src, dst, send, recv, k):
        return pltpu.make_async_remote_copy(
            src_ref=src,
            dst_ref=dst,
            send_sem=send,
            recv_sem=recv,
            device_id={"hidden": partner[k]},
            device_id_type=MESH,
        )

    def forward_copy(k, c):
        return to_hidden(U[k][c], R[k][c], fs.at[k, c], fr.at[k, c], k)

    def backward_copy(k, c):
        way = (L - 1 - k) % 2
        return to_hidden(S[way][c], Tt[way][c], bs.at[k, c], br.at[k, c], k)

    queues = [[(way, c) for way in (forward_copy, backward_copy) for c in range(C)] for _ in range(L)]
    made, landed, sent = [set() for _ in range(L)], [0] * L, [0] * L

    def move_on(k):
        while sent[k] < 2 * C and queues[k][sent[k]] in made[k] and sent[k] - WINDOW[min(k, 2)] < landed[k]:
            way, c = queues[k][sent[k]]
            way(k, c).start()
            sent[k] += 1

    def send(k, way, c):
        made[k].add((way, c))
        move_on(k)

    def receive(k, way, c):
        assert queues[k][landed[k]] == (way, c) and sent[k] > landed[k]
        way(k, c).wait_recv()
        landed[k] += 1
        move_on(k)

    def sum_copy(i, k, mine, inbox):
        return to_hidden(mine.at[k], inbox.at[k], ps.at[i, k], pr.at[i, k], k)

    def to_dp(i, off, src, dst):
        return pltpu.make_async_remote_copy(
            src_ref=src,
            dst_ref=dst,
            send_sem=rs.at[i, off - 1],
            recv_sem=rr.at[i, off - 1],
            device_id={"dp": peers[off - 1]},
            device_id_type=MESH,
        )

    out_share, in_share = out_parts.shape[1], in_parts.shape[1]

    def level_copy(k, off):
        return to_dp(k, off, lg.at[k % 2, peers[off - 1]], level_parts.at[k, off])

    def in_rows(at):
        return pl.ds(pl.multiple_of(at * in_share, 16), in_share)

    def out_rows(at):
        return pl.ds(pl.multiple_of(at * out_share, 16), out_share)

    bits = N.bit_length() - 1
    own_bit = [lax.rem(dp // 2**b, 2) for b in range(bits)]
    half = NB // 4 * 256

    def shares(side, step):
        ways = list(range(bits)) if side == 0 else list(reversed(range(bits)))
        b, rest = ways[step], ways[step + 1 :]
        fixed = sum((own_bit[p] * 2**p for p in ways[:step]), 0)
        free = [0]
        for q in rest:
            free = free + [f + 2**q for f in free]
        give = [fixed + (1 - own_bit[b]) * 2**b + f for f in free]
        keep = [fixed + own_bit[b] * 2**b + f for f in free]
        return give, keep, dp + 2**b - 2 * 2**b * own_bit[b]

    def seat(step, i):
        return sum(N >> (p + 1) for p in range(step)) + i

    def side_columns(side):
        return pl.ds(side * half, half)

    def half_copy(side, step, i):
        give, _, other = shares(side, step)
        last = step == bits - 1
        return pltpu.make_async_remote_copy(
            src_ref=w_in.at[in_rows(give[i]), side_columns(side)],
            dst_ref=in_parts.at[1, :, side_columns(side)] if last else arrived[side].at[seat(step, i)],
            send_sem=hs.at[side, seat(step, i)],
            recv_sem=hr.at[side, seat(step, i)],
            device_id={"dp": other},
            device_id_type=MESH,
        )

    def out_copy(off):
        return to_dp(L, off, w_out.at[out_rows(peers[off - 1])], out_parts.at[off])

    own_copies = [pltpu.make_async_copy(lg.at[k % 2, dp], level_parts.at[k, 0], own_sem.at[k]) for k in range(L)]
    own_copies.append(pltpu.make_async_copy(w_in.at[in_rows(dp)], in_parts.at[0], own_sem.at[L]))
    own_copies.append(pltpu.make_async_copy(w_out.at[out_rows(dp)], out_parts.at[0], own_sem.at[L + 1]))

    def rows(c):
        return pl.ds(begins[c], sizes[c])

    tiles = [pl.ds(at, LANES) for at in range(0, T, LANES)]

    def as_row(column):
        return jnp.broadcast_to(column, (LANES, LANES)).T[:SUB]

    def as_column(row):
        return jnp.broadcast_to(row[:1], (LANES, LANES)).T

    def groups(most, body, count=NB):
        size = max(n for n in range(1, most + 1) if count % n == 0)

        def step(i, carry):
            body([size * i + b for b in range(size)])
            return carry

        lax.fori_loop(0, count // size, step, 0)

    def pairs(most, body):
        groups(most, body, NB // 2)

    def wide_columns(i, width):
        return pl.ds(pl.multiple_of(i * width, width), width)

    need(0)
    for tile in tiles:
        x = tok[tile, :].astype(WIDE)
        squares[0, :, tile] = as_row(jnp.sum(x * x, axis=1, keepdims=True))
    pl.semaphore_wait(barrier, L + N - 1)
    for k in range(L):
        copy = sum_copy(0, k, squares, squares_in)
        copy.start()
        copy.wait()
        squares[k + 1] = squares[k] + squares_in[k]
    for tile in tiles:
        mean = squares[L, :, tile] / total_features
        recip[tile, :] = as_column(lax.rsqrt(mean + 1e-06))

    def start(_, c):
        need(1)
        here = pl.ds(0, sizes[c])
        xs[here, :] = (tok[rows(c), :].astype(WIDE) * recip[rows(c), :1]).astype(NARROW)

        def body(these):
            made = [nn(xs[here, :], w_in[:, wide_columns(i, 256)]).astype(NARROW) for i in these]
            for i, wide in zip(these, made):
                U[0][c][2 * i] = wide[:, :128]
                U[0][c][2 * i + 1] = wide[:, 128:]

        pairs(GROUP[0], body)
        send(0, forward_copy, c)

    def mixed(k, c, j):
        both = jnp.concatenate([U[k][c][j], R[k][c][order[k, j]]], axis=1)
        return nn(both, lw[k, j].reshape(256, 128)).astype(NARROW)

    def forward(k, c):
        need(2)
        receive(k, forward_copy, c)
        if k < L - 1:

            def body(these):
                made = [mixed(k, c, j) for j in these]
                for j, value in zip(these, made):
                    U[k + 1][c][j] = value

            groups(GROUP[1], body)
            send(k + 1, forward_copy, c)
            return
        need(3, 4)

        def body(these):
            blocks = [(n, b, 2 * i + b) for n, i in enumerate(these) for b in range(2)]
            tops = [mixed(k, c, j) for _, _, j in blocks]
            d_act = [nt(cot[rows(c), :], w_out[wide_columns(i, 256), :]) for i in these]
            values, grads = [], []
            for (n, b, _), top in zip(blocks, tops):
                value, slope = gelu_pair(top.astype(WIDE))
                values.append(value.astype(NARROW))
                grads.append((d_act[n][:, b * 128 : (b + 1) * 128] * slope).astype(NARROW))
            going = [nt(g, lw[k, j, 1]).astype(NARROW) for g, (_, _, j) in zip(grads, blocks)]
            for (_, _, j), value, g, s in zip(blocks, values, grads, going):
                act[c][j] = value
                G[0][c][j] = g
                S[0][c][j] = s

        pairs(GROUP[2], body)
        send(k, backward_copy, c)

    def output(_, c):
        here = pl.ds(0, sizes[c])
        slot = len(out_stores) % 2
        if len(out_stores) >= 2:
            out_stores[-2].wait()
        dn[here, :] = jnp.zeros((sizes[c], Dl), WIDE)

        def step(q, carry):
            wide = jnp.concatenate([act[c][4 * q + b] for b in range(4)], axis=1)
            dn[here, :] += nn(wide, w_out[wide_columns(q, 512), :])
            return carry

        lax.fori_loop(0, NB // 4, step, 0)
        ost[slot, here, :] = dn[here, :].astype(NARROW)
        out_stores.append(pltpu.make_async_copy(ost.at[slot, here], out_hbm.at[rows(c)], store_sem.at[1 + slot]))
        out_stores[-1].start()

    def all_rows(ref, j):
        return jnp.concatenate([ref[c][j] for c in range(C)], axis=0)

    def all_pair(ref, i):
        return jnp.concatenate([all_rows(ref, 2 * i), all_rows(ref, 2 * i + 1)], axis=1)

    token_store = pltpu.make_async_copy(tok, token_grad_hbm, store_sem.at[0])

    def output_grad(_, __):
        for tile in tiles:
            x = (tok[tile, :].astype(WIDE) * recip[tile, :1]).astype(NARROW)
            norm_t[:, tile] = x.astype(WIDE).T.astype(NARROW)

        def body(these):
            made = [tn(all_pair(act, i), cot[...]).astype(NARROW) for i in these]
            for i, value in zip(these, made):
                w_out[wide_columns(i, 256), :] = value

        pairs(GROUP[3], body)
        for off in range(1, N):
            out_copy(off).start()
        own_copies[L + 1].start()

    def level_grad(k, _):
        share = 128 // N
        if k + 2 < L:
            for off in range(1, N):
                level_copy(k + 2, off).wait_send()
            own_copies[k + 2].wait()

        def one(j):
            theirs = jnp.concatenate([R[k][c][order[k, j]] for c in range(C)], axis=0)
            both = jnp.concatenate([all_rows(U[k], j), theirs], axis=1)
            return tn(both, all_rows(G[(L - 1 - k) % 2], j)).astype(NARROW)

        def body(these):
            made = [one(j) for j in these]
            for j, value in zip(these, made):
                for r in range(N):
                    for b in range(2):
                        lg[k % 2, r, j, b] = value[b * 128 + r * share : b * 128 + (r + 1) * share]

        groups(GROUP[4], body)
        for off in range(1, N):
            level_copy(k, off).start()
        own_copies[k].start()

    def backward(k, c):
        receive(k, backward_copy, c)
        if 0 < k < L - 1:
            backward_copy(k + 1, c).wait_send()
        upper, lower = G[(L - 1 - k) % 2], G[(L - k) % 2] if k else U[L - 1]
        if k == 0:
            forward_copy(L - 1, c).wait_send()
        came = Tt[(L - 1 - k) % 2][c]
        going = S[(L - k) % 2]

        def body(these):
            own = [nt(upper[c][j], lw[k, j, 0]) for j in these]
            grads = [(o + came[inverse[k, j]].astype(WIDE)).astype(NARROW) for o, j in zip(own, these)]
            leave = [nt(g, lw[k - 1, j, 1]).astype(NARROW) for g, j in zip(grads, these)] if k > 0 else []
            for j, g in zip(these, grads):
                lower[c][j] = g
            for j, value in zip(these, leave):
                going[c][j] = value

        groups(GROUP[5], body)
        if k >= 2:
            pl.semaphore_signal(
                credit.at[k - 2, c], inc=1, device_id={"hidden": partner[k - 2]}, device_id_type=MESH
            )
        if k > 0:
            if k - 1 <= L - 3:
                pl.semaphore_wait(credit.at[k - 1, c], 1)
            send(k - 1, backward_copy, c)
            return
        dn[rows(c), :] = jnp.zeros((sizes[c], Dl), WIDE)

        def step(q, carry):
            wide = jnp.concatenate([lower[c][4 * q + b] for b in range(4)], axis=1)
            dn[rows(c), :] += nt(wide, w_in[:, wide_columns(q, 512)])
            return carry

        lax.fori_loop(0, NB // 4, step, 0)
        for tile in tiles:
            if begins[c] < tile.start + LANES <= begins[c] + sizes[c]:
                dots = jnp.sum(dn[tile, :] * tok[tile, :].astype(WIDE), axis=1, keepdims=True)
                inner[0, :, tile] = as_row(dots)

    doing = dict(
        start=start,
        forward=forward,
        output=output,
        output_grad=output_grad,
        level_grad=level_grad,
        backward=backward,
    )
    for name, k, c in schedule(L, C):
        if (name, k) != ("level_grad", 0):
            doing[name](k, c)

    first = U[L - 1]

    def in_grad(at, side):
        def body(these):
            these = [i + side * (NB // 4) for i in these]
            made = [nn(norm_t[in_rows(at), :], all_pair(first, i)).astype(NARROW) for i in these]
            for i, value in zip(these, made):
                w_in[in_rows(at), wide_columns(i, 256)] = value

        groups(GROUP[6], body, NB // 4)

    hops = iter(range(L))

    def hop():
        k = next(hops, None)
        if k is not None:
            sum_copy(1, k, inner, inner_in).wait()
            inner[k + 1] = inner[k] + inner_in[k]
            if k + 1 < L:
                sum_copy(1, k + 1, inner, inner_in).start()

    sum_copy(1, 0, inner, inner_in).start()
    for i in range(N // 2):
        for side in range(2):
            in_grad(shares(side, 0)[0][i], side)
            half_copy(side, 0, i).start()
        hop()
    for i in range(N // 2):
        for side in range(2):
            in_grad(shares(side, 0)[1][i], side)
        hop()
    level_grad(0, 0)
    for _ in range(L):
        hop()
    for tile in tiles:
        mean = as_column(inner[L, :, tile] / total_features)[:, :1]
        scale = recip[tile, :1]
        cube = scale * scale * scale
        wide = tok[tile, :].astype(WIDE)
        tok[tile, :] = (scale * dn[tile, :] - wide * (cube * mean)).astype(NARROW)
    token_store.start()
    for step in range(bits - 1):
        count = N >> (step + 1)
        for i in range(count):
            for side in range(2):
                half_copy(side, step, i).wait()
                rows_here = in_rows(shares(side, step)[1][i])
                columns = side_columns(side)
                more = arrived[side][seat(step, i)].astype(WIDE)
                w_in[rows_here, columns] = (w_in[rows_here, columns].astype(WIDE) + more).astype(NARROW)
        for i in range(count // 2):
            for side in range(2):
                half_copy(side, step + 1, i).start()
    own_copies[L].start()

    for k in range(L):
        for c in range(C):
            if k < L - 1:
                forward_copy(k, c).wait_send()
            if k < 2:
                backward_copy(k, c).wait_send()
    for off in range(1, N):
        for k in range(L):
            level_copy(k, off).wait_recv()
            if k < 2:
                level_copy(k, off).wait_send()
        out_copy(off).wait()
    for side in range(2):
        half_copy(side, bits - 1, 0).wait()
    for copy in own_copies[:2] + own_copies[L:]:
        copy.wait()
    for copy in out_stores[-2:]:
        copy.wait()
    token_store.wait()


def local(sizes, tokens, cotangent, weight_in, level_weights, weight_out, block_order):
    N, H = sizes
    T, Dl = tokens.shape
    L, NB = block_order.shape
    F = weight_in.shape[1]
    BLK = level_weights.shape[-1]
    chunks = chunk_rows(T)
    C, most = len(chunks), max(chunks)
    grad_scale = 1.0 / math.sqrt(T * N)
    seats = jnp.arange(NB, dtype=jnp.int32)
    inverse = jnp.sum(
        jnp.where(block_order[:, :, None] == seats[None, None, :], seats[None, :, None], 0), axis=1, dtype=jnp.int32
    )
    scratch = [pltpu.VMEM((NB, rows, BLK), NARROW) for rows in chunks] * (2 * L + 6)
    scratch += [
        pltpu.VMEM(a.shape, a.dtype) for a in (tokens, cotangent, weight_in, level_weights, weight_out)
    ]
    scratch += [
        pltpu.VMEM((T, LANES), WIDE),
        pltpu.VMEM((Dl, T), NARROW),
        pltpu.VMEM((most, Dl), NARROW),
        pltpu.VMEM((T, Dl), WIDE),
        pltpu.VMEM((2, most, Dl), NARROW),
        pltpu.VMEM((2, N, NB, 2, BLK // N, BLK), NARROW),
    ]
    scratch += [pltpu.VMEM((count, SUB, T), WIDE) for count in (L + 1, L, L + 1, L)]
    scratch += [pltpu.VMEM((max(N - 2, 1), Dl // N, F // 2), NARROW)] * 2
    dma = pltpu.SemaphoreType.DMA
    scratch += [dma((5,))] + [dma((L, C))] * 4 + [dma((2, L))] * 2 + [dma((L + 1, N - 1))] * 2 + [dma((2, N - 1))] * 2 + [dma((L + 2,))]
    scratch += [pltpu.SemaphoreType.REGULAR((max(L - 2, 1), C)), dma((3,))]
    outs = (
        jax.ShapeDtypeStruct((T, Dl), NARROW),
        jax.ShapeDtypeStruct((T, Dl), NARROW),
        jax.ShapeDtypeStruct((L, N, NB, 2, BLK // N, BLK), NARROW),
        jax.ShapeDtypeStruct((2, Dl // N, F), NARROW),
        jax.ShapeDtypeStruct((N, F // N, Dl), NARROW),
    )
    plan = (L, N, chunks, Dl, NB, Dl * H)
    result, token_grad, level_parts, in_parts, out_parts = pl.pallas_call(
        functools.partial(layer, plan),
        out_shape=outs,
        in_specs=[pl.BlockSpec(memory_space=pltpu.SMEM)] * 2 + [pl.BlockSpec(memory_space=pl.ANY)] * 5,
        out_specs=[pl.BlockSpec(memory_space=pl.ANY)] * 5,
        scratch_shapes=scratch,
        compiler_params=pltpu.CompilerParams(
            collective_id=0, has_side_effects=True, vmem_limit_bytes=63 * 2**20
        ),
        cost_estimate=pl.CostEstimate(flops=18 * T * Dl * F, bytes_accessed=30 * 2**20, transcendentals=T * F),
    )(block_order, inverse, tokens, cotangent, weight_in, level_weights, weight_out)

    def total(parts, axis):
        split = [lax.index_in_dim(parts, i, axis, keepdims=False) for i in range(parts.shape[axis])]
        return functools.reduce(jnp.add, [s.astype(WIDE) for s in split]) * grad_scale

    return result, token_grad, total(level_parts, 1), total(in_parts, 0), total(out_parts, 0)


def solution(mesh):
    sizes = (mesh.shape["dp"], mesh.shape["hidden"])
    in_specs = (
        P("dp", "hidden"),
        P("dp", "hidden"),
        P("hidden", None),
        P(None, "hidden", None, None, None),
        P("hidden", None),
        P(),
    )
    out_specs = (
        P("dp", "hidden"),
        P("dp", "hidden"),
        P(None, "hidden", None, "dp", None),
        P(("hidden", "dp"), None),
        P(("hidden", "dp"), None),
    )
    return jax.shard_map(
        functools.partial(local, sizes), mesh=mesh, in_specs=in_specs, out_specs=out_specs, check_vma=False
    )
```
